32 devices in a mesh: ctx: 8 (over y, x, core), head: 4 (over z).
Axes of the slice: x: 2, y: 2, z: 4, core: 2. Of those that a mesh axis runs over, the one named last changes fastest.
Arguments:
- latent_keys: bfloat16 [1024, 576], P('ctx'), may hold values from -6 to 6
- index_keys: bfloat16 [1024, 128], P('ctx'), may hold values from -6 to 6
- main_query: bfloat16 [1024, 73728], P('ctx', 'head'), may hold values from -107 to 107
- index_query: bfloat16 [1024, 8192], P('ctx', 'head'), may hold values from -10 to 10
- index_weight: bfloat16 [1024, 64], P('ctx', 'head'), may hold values from 0.029907227 to 0.29882812
- segment_ids: int32 [1024], replicated, may hold values from 0 to 7, never falling along the last dimension, each value on 1 to 256 neighbouring positions
- block_order: int32 [16], replicated, may hold values from 0 to 15, each once
Outputs:
- kl: float32 [1024], P('ctx')
The draws below stay inside these ranges and needn't reach their ends.
Inputs may be any that keep to these rules, and one draw needn't show every extreme that they name: `segment_ids`: never falls along the sequence; each document holds 1 to 256 positions and one holds exactly that many. `block_order`: each block number appears once.
All inputs are finite; a program needn't handle non-finite values.
Results may differ from the reference program's by a relative error of at most 0.0003.
Values may be sent and summed in bfloat16 or wider, within the bound.
No kernel may reach another device: no remote copies, remote signals or barrier semaphores. Data moves between devices by JAX's collectives and lax.ppermute only.
A program may use at most 64 MiB of HBM per device.

```python
import math
import jax
import jax.numpy as jnp
import numpy as np
from jax import lax

HEADS = 128
IHEADS = 64
IDIM = 128
KDIM = 576
HALF = 64
SEQ = 1024
N_CTX = 8


def latent_table(key):
    noise = jax.random.normal(jax.random.fold_in(key, 101), (SEQ, KDIM), jnp.float32)
    return jnp.clip(noise, -6.0, 6.0)


def index_table(key):
    noise = jax.random.normal(jax.random.fold_in(key, 202), (SEQ, IDIM), jnp.float32)
    return jnp.clip(noise, -6.0, 6.0)


def drawn_flags(key):
    return jnp.arange(SEQ) % 16 == 0


def draw_latent_keys(key, part):
    return latent_table(key).astype(jnp.bfloat16)


def draw_index_keys(key, part):
    return index_table(key).astype(jnp.bfloat16)


def draw_main_query(key, part):
    noise = jax.random.normal(jax.random.fold_in(key, 404), (SEQ, HEADS, KDIM), jnp.float32)
    values = jnp.clip(noise, -6.0, 6.0)
    target_score = 120.0 + 200.0 * jax.random.uniform(jax.random.fold_in(key, 405), (SEQ, HEADS), jnp.float32)
    factor = target_score * 192.0 ** 0.5 / KDIM
    copied = factor[:, :, None] * latent_table(key)[:, None, :]
    values = jnp.where(drawn_flags(key)[:, None, None], copied, values)
    bound = 48.0 + float(34000 // KDIM)
    values = jnp.clip(values, -bound, bound)
    return values.reshape(SEQ, HEADS * KDIM).astype(jnp.bfloat16)


def draw_index_query(key, part):
    noise = jax.random.normal(jax.random.fold_in(key, 505), (SEQ, IHEADS, IDIM), jnp.float32)
    values = jnp.clip(noise, -6.0, 6.0) * IDIM ** (-0.5)
    target_score = 120.0 + 200.0 * jax.random.uniform(jax.random.fold_in(key, 506), (SEQ,), jnp.float32)
    factor = target_score / (IDIM * IHEADS * 0.117)
    copied = factor[:, None, None] * index_table(key)[:, None, :]
    values = jnp.where(drawn_flags(key)[:, None, None], copied, values)
    bound = 3.0 + float(60000 // (IDIM * IHEADS))
    values = jnp.clip(values, -bound, bound)
    return values.reshape(SEQ, IHEADS * IDIM).astype(jnp.bfloat16)


def steps_of(stream_key, shape, split, low, largest):
    level, own = 1.0, jax.random.fold_in(stream_key, 6)
    for axis_at, parts in split:
        steps = jnp.exp(jax.random.uniform(jax.random.fold_in(own, axis_at), (parts,), jnp.float32, low / len(split), largest / len(split)))
        level = level * jnp.repeat(steps, shape[axis_at] // parts).reshape([-1 if axis == axis_at else 1 for axis in range(len(shape))])
    return level


def profile(amount, total, reach, skew):
    weights = [(1 << 20) // math.isqrt(rank ** skew) + 1 for rank in range(2, amount + 1)]
    surplus, holding = total - reach - (amount - 1), [1] * (amount - 1)
    while surplus > 0:
        candidates = [i for i in range(amount - 1) if holding[i] < reach]
        mass, left = sum([weights[i] for i in candidates]), surplus
        for i in candidates:
            addition = min(reach - holding[i], max(1, left * weights[i] // mass), surplus)
            holding[i] = holding[i] + addition
            surplus = surplus - addition
    return np.array([reach] + holding)


def ragged_sizes(rng, number_of, total, most, slope):
    if number_of == 2:
        one = jax.random.randint(rng, (), max(1, total - most), min(most, total - 1) + 1)
        return jnp.stack([one, total - one])
    lengths = jnp.asarray(profile(number_of, total, most, slope), jnp.int32)
    couples = (number_of - 1) // 2
    donor, receiver = lengths[1:1 + 2 * couples:2], lengths[2:2 + 2 * couples:2]
    margin = jnp.minimum(donor - 1, most - receiver)
    moved = jax.random.randint(jax.random.fold_in(rng, 1), (couples,), 0, 1 << 20) % (margin + 1)
    lengths = lengths.at[1:1 + 2 * couples:2].set(donor - moved).at[2:2 + 2 * couples:2].set(receiver + moved)
    return lengths[jax.random.permutation(jax.random.fold_in(rng, 2), number_of)]


def setup_inputs(seed: int = 0) -> dict:
    key_of = jax.random.split(jax.random.key(seed), 8)
    return {
        "latent_keys": draw_latent_keys(jax.random.fold_in(key_of[7], 71), 0),
        "index_keys": draw_index_keys(jax.random.fold_in(key_of[7], 71), 0),
        "main_query": draw_main_query(jax.random.fold_in(key_of[7], 71), 0),
        "index_query": draw_index_query(jax.random.fold_in(key_of[7], 71), 0),
        "index_weight": jnp.clip(jnp.exp(math.log(0.29882812) - 2.30176843 * jax.random.uniform(key_of[4], (SEQ, IHEADS), jnp.float32) ** steps_of(key_of[4], (SEQ, IHEADS), ((0, 8), (1, 4)), -0.2, 0.2)), 0.029907227, 0.29882812).astype(jnp.bfloat16),
        "segment_ids": jnp.searchsorted(jnp.cumsum(ragged_sizes(key_of[5], 8, SEQ, SEQ // 4, 2)), jnp.arange(SEQ), side="right").astype(jnp.int32),
        "block_order": jax.random.permutation(key_of[6], 2 * N_CTX).astype(jnp.int32),
    }


score_scale = 192.0 ** -0.5
masked_fill = -1e30


def key_positions(block_order, half_block):
    offsets = jnp.arange(half_block, dtype=jnp.int32)
    return (block_order[:, None] * half_block + offsets[None, :]).reshape(-1).astype(jnp.int32)


def visible_mask(query_pos, key_pos, segment_ids):
    query_seg = jnp.take(segment_ids, query_pos)
    key_seg = jnp.take(segment_ids, key_pos)
    return (key_pos[None, :] <= query_pos[:, None]) & (key_seg[None, :] == query_seg[:, None])


def head_scores(query_head, key_table):
    raw = lax.dot_general(query_head, key_table, (((1,), (1,)), ((), ())), preferred_element_type=jnp.float32)
    return raw * score_scale


def softmax_add(running, scores, visible):
    masked = jnp.where(visible, scores, masked_fill)
    row_max = jnp.max(masked, axis=1, keepdims=True)
    powers = jnp.where(visible, jnp.exp(masked - row_max), 0.0)
    return running + powers / jnp.sum(powers, axis=1, keepdims=True)


def index_scores(query_rows, gains, key_table):
    row_count = query_rows.shape[0]
    head_count = gains.shape[1]
    head_width = query_rows.shape[1] // head_count
    stacked = jnp.moveaxis(query_rows.reshape(row_count, head_count, head_width), 1, 0)
    gain_rows = jnp.moveaxis(gains.astype(jnp.float32), 1, 0)

    def add_head(running, pieces):
        query_head, gain_head = pieces
        dots = lax.dot_general(query_head, key_table, (((1,), (1,)), ((), ())), preferred_element_type=jnp.float32)
        return running + gain_head[:, None] * jnp.maximum(dots, 0.0), None

    start_sum = jnp.zeros((row_count, key_table.shape[0]), jnp.float32)
    running, _ = lax.scan(add_head, start_sum, (stacked, gain_rows))
    return running


def row_terms(target, index_score, visible):
    masked = jnp.where(visible, index_score, masked_fill)
    row_max = jnp.max(masked, axis=1)
    exp_sum = jnp.sum(jnp.where(visible, jnp.exp(masked - row_max[:, None]), 0.0), axis=1)
    positive = target > 0.0
    safe_target = jnp.where(positive, target, 1.0)
    entropy_sum = jnp.sum(jnp.where(positive, target * jnp.log(safe_target), 0.0), axis=1)
    cross_sum = jnp.sum(jnp.where(visible, target * index_score, 0.0), axis=1)
    target_sum = jnp.sum(target, axis=1)
    return row_max, exp_sum, entropy_sum, cross_sum, target_sum


def finish_rows(row_max, exp_sum, entropy_sum, cross_sum, target_sum):
    return entropy_sum - cross_sum + (row_max + jnp.log(exp_sum)) * target_sum


def reference(latent_keys, index_keys, main_query, index_query, index_weight, segment_ids, block_order):
    key_pos = key_positions(block_order, HALF)
    visible = visible_mask(key_pos, key_pos, segment_ids)
    stacked = jnp.moveaxis(main_query.reshape(SEQ, HEADS, KDIM), 1, 0)

    def add_head(running, query_head):
        return softmax_add(running, head_scores(query_head, latent_keys), visible), None

    running, _ = lax.scan(add_head, jnp.zeros((SEQ, SEQ), jnp.float32), stacked)
    target = running / HEADS
    index_score = index_scores(index_query, index_weight, index_keys)
    row_max, exp_sum, entropy_sum, cross_sum, target_sum = row_terms(target, index_score, visible)
    return finish_rows(row_max, exp_sum, entropy_sum, cross_sum, target_sum)
```

```python
import functools
import math

import jax
import jax.numpy as jnp
from jax import lax
from jax.experimental import pallas as pl
from jax.experimental.pallas import tpu as pltpu
from jax.sharding import PartitionSpec as P

LANES = 128
score_scale = 192.0 ** (-0.5)
hidden = -1e30


def swap(x, axis, distance):
    size = lax.axis_size(axis)
    return lax.ppermute(x, axis, [(i, i ^ distance) for i in range(size)])


def window_masks(block, reach, half, seg_ref):
    table_rows = seg_ref.shape[0]
    first = block - reach // half
    row0 = lax.div(first + 2 * table_rows, 2) - table_rows
    pieces = []
    for k in range(reach // LANES + 2):
        row = jnp.clip(row0 + k, 0, table_rows - 1)
        pieces.append(seg_ref[pl.ds(row, 1), :].astype(jnp.float32))
    wide = jnp.concatenate(pieces, axis=1)
    width = wide.shape[1]
    moved = pltpu.roll(wide, width - half, 1)
    odd = lax.rem(first + 2 * table_rows, 2)
    wide = jnp.where(odd == 1, moved, wide)
    tail_seg = jnp.broadcast_to(wide[:, reach : reach + LANES], (half, LANES))
    head_seg = jnp.broadcast_to(wide[:, :LANES], (half, LANES))
    row_id = lax.broadcasted_iota(jnp.int32, (half, LANES), 0)
    lane_id = lax.broadcasted_iota(jnp.int32, (half, LANES), 1)
    query_seg = jnp.sum(jnp.where(row_id == lane_id, tail_seg, 0.0), axis=1, keepdims=True)
    in_tail = lane_id <= row_id
    in_tail = in_tail & (lane_id < half)
    key_seg = jnp.concatenate(
        [jnp.where(in_tail, tail_seg, head_seg), jnp.broadcast_to(wide[:, LANES:reach], (half, reach - LANES))], axis=1
    )
    place = lax.broadcasted_iota(jnp.int32, (half, reach), 1)
    rows_full = lax.broadcasted_iota(jnp.int32, (half, reach), 0)
    tail_full = (place <= rows_full) & (place < half)
    position = first * half + place + jnp.where(tail_full, reach, 0)
    visible = (key_seg == query_seg) & (position >= 0)
    return in_tail, visible


def ring_fold(in_tail, wide, reach):
    low = jnp.where(in_tail, wide[:, reach : reach + LANES], wide[:, :LANES])
    return jnp.concatenate([low, wide[:, LANES:reach]], axis=1)


def slot_table(order_ref, inverse_ref):
    for slot in range(order_ref.shape[0]):
        inverse_ref[order_ref[slot]] = slot


def build_window(order_ref, inverse_ref, stack_ref, block, reach, half, store):
    first = block - reach // half
    for w in range(reach // half + 1):
        slot = inverse_ref[jnp.maximum(first + w, 0)]
        store(w, pl.multiple_of(slot * half, half))


def index_kernel(sizes, order_ref, seg_ref, query_ref, weight_ref, *refs):
    n_ctx, rows, half, reach, key_pad = sizes
    piece_refs, (out_ref, stack_ref, window_ref, inverse_ref) = refs[:n_ctx], refs[n_ctx:]
    me = lax.axis_index("ctx")
    for s in range(n_ctx):
        start = pl.multiple_of((me ^ s) * rows, rows)
        stack_ref[pl.ds(start, rows), :] = piece_refs[s][:, key_pad:]
    slot_table(order_ref, inverse_ref)
    idim = stack_ref.shape[1]
    heads = query_ref.shape[1] // idim
    weights = jnp.transpose(weight_ref[...].astype(jnp.float32), (1, 0))
    together = 4
    for i in range(rows // half):
        block = order_ref[me * (rows // half) + i]

        def store(w, at):
            window_ref[w * half : (w + 1) * half, :] = stack_ref[pl.ds(at, half), :]

        build_window(order_ref, inverse_ref, stack_ref, block, reach, half, store)
        window_ref[reach + half :, :] = jnp.zeros((window_ref.shape[0] - reach - half, idim), window_ref.dtype)
        in_tail, visible = window_masks(block, reach, half, seg_ref)
        total = jnp.zeros((half, reach), jnp.float32)
        for j0 in range(0, heads, together):
            lhs = jnp.concatenate(
                [query_ref[i * half : (i + 1) * half, j * idim : (j + 1) * idim] for j in range(j0, j0 + together)], axis=0
            )
            dots = lax.dot_general(
                lhs, window_ref[...], (((1,), (1,)), ((), ())), preferred_element_type=jnp.float32
            )
            for k in range(together):
                folded = ring_fold(in_tail, dots[k * half : (k + 1) * half, :], reach)
                gain = weights[i * half : (i + 1) * half, j0 + k : j0 + k + 1]
                total = total + gain * jnp.maximum(folded, 0.0)
        out_ref[i * half : (i + 1) * half, :] = jnp.where(visible, total, 0.0)


def target_kernel(sizes, order_ref, seg_ref, query_ref, *refs):
    n_ctx, rows, half, reach, key_pad, key_width = sizes
    piece_refs = refs[:n_ctx]
    out_ref, stack_ref, even_ref, odd_ref, bias_ref, inverse_ref = refs[n_ctx:]
    me = lax.axis_index("ctx")
    wide = even_ref.shape[1]

    @pl.when(pl.program_id(0) == 0)
    def _():
        for s in range(n_ctx):
            start = pl.multiple_of((me ^ s) * rows, rows)
            stack_ref[pl.ds(start, rows), :] = piece_refs[s][:, :key_pad]
        slot_table(order_ref, inverse_ref)
        for i in range(rows // half):
            block = order_ref[me * (rows // half) + i]

            def store(w, at):
                piece = stack_ref[pl.ds(at, half), :]
                even_ref[i, w * half : (w + 1) * half, :] = piece
                turned = pltpu.roll(piece.astype(jnp.float32), key_pad - key_width, 1)
                odd_ref[i, w * half : (w + 1) * half, :] = turned.astype(piece.dtype)

            build_window(order_ref, inverse_ref, stack_ref, block, reach, half, store)
            blank = jnp.zeros((wide - reach - half, key_pad), even_ref.dtype)
            even_ref[i, reach + half :, :] = blank
            odd_ref[i, reach + half :, :] = blank
            _, visible = window_masks(block, reach, half, seg_ref)
            bias_ref[i] = jnp.where(visible, 0.0, hidden)
        out_ref[...] = jnp.zeros_like(out_ref)

    heads = query_ref.shape[1] // key_width
    row_id = lax.broadcasted_iota(jnp.int32, (half, LANES), 0)
    lane_id = lax.broadcasted_iota(jnp.int32, (half, LANES), 1)
    in_tail = (lane_id <= row_id) & (lane_id < half)
    for i in range(rows // half):
        for parity, keys_ref in ((0, even_ref), (1, odd_ref)):
            starts = [g * 2 * key_width + parity * (2 * key_width - key_pad) for g in range(heads // 2)]
            lhs = jnp.concatenate(
                [query_ref[i * half : (i + 1) * half, at : at + key_pad] for at in starts], axis=0
            )
            raw = lax.dot_general(
                lhs, keys_ref[i], (((1,), (1,)), ((), ())), preferred_element_type=jnp.float32
            )
            for g in range(heads // 2):
                scores = ring_fold(in_tail, raw[g * half : (g + 1) * half, :], reach) + bias_ref[i]
                row_max = jnp.max(scores, axis=1, keepdims=True)
                powers = jnp.exp2((scores - row_max) * (score_scale * math.log2(math.e)))
                share = 1.0 / jnp.sum(powers, axis=1, keepdims=True)
                out_ref[i * half : (i + 1) * half, :] += powers * share


def loss_kernel(sizes, order_ref, seg_ref, *refs):
    rows, half, reach, total_heads = sizes
    target_refs, index_refs, out_ref = refs[:2], refs[2:4], refs[4]
    me = lax.axis_index("ctx")
    columns = []
    for i in range(rows // half):
        block = order_ref[me * (rows // half) + i]
        _, visible = window_masks(block, reach, half, seg_ref)
        here = slice(i * half, (i + 1) * half)
        target = (target_refs[0][here, :] + target_refs[1][here, :]) * (1.0 / total_heads)
        index_score = index_refs[0][here, :] + index_refs[1][here, :]
        masked = jnp.where(visible, index_score, hidden)
        row_max = jnp.max(masked, axis=1, keepdims=True)
        exp_sum = jnp.sum(jnp.where(visible, jnp.exp(masked - row_max), 0.0), axis=1, keepdims=True)
        positive = target > 0.0
        logs = jnp.log(jnp.where(positive, target, 1.0))
        entropy_sum = jnp.sum(jnp.where(positive, target * logs, 0.0), axis=1, keepdims=True)
        cross_sum = jnp.sum(jnp.where(visible, target * index_score, 0.0), axis=1, keepdims=True)
        target_sum = jnp.sum(target, axis=1, keepdims=True)
        columns.append(entropy_sum - cross_sum + (row_max + jnp.log(exp_sum)) * target_sum)
    column = jnp.concatenate(columns, axis=0)
    row_id = lax.broadcasted_iota(jnp.int32, (rows, rows), 0)
    lane_id = lax.broadcasted_iota(jnp.int32, (rows, rows), 1)
    out_ref[...] = jnp.sum(jnp.where(row_id == lane_id, column, 0.0), axis=0, keepdims=True)


def per_device(
    latent_keys, index_keys, main_query, index_query, index_weight, segment_ids, block_order
):
    n_ctx, n_head = lax.axis_size("ctx"), lax.axis_size("head")
    rows, key_width = latent_keys.shape
    idim = index_keys.shape[1]
    seq_len = segment_ids.shape[0]
    half = seq_len // block_order.shape[0]
    reach = seq_len // 4
    heads = main_query.shape[1] // key_width
    key_pad = -(-key_width // LANES) * LANES
    wide = reach + LANES

    packed = jnp.concatenate(
        [latent_keys, jnp.zeros((rows, key_pad - key_width), latent_keys.dtype), index_keys], axis=1
    )
    own_core = [packed] + [swap(packed, "ctx", 2 * s) for s in range(1, n_ctx // 2)]
    pieces = []
    for piece in own_core:
        pieces += [piece, swap(piece, "ctx", 1)]
    seg_table = segment_ids.reshape(seq_len // LANES, LANES)

    vmem = pl.BlockSpec(memory_space=pltpu.VMEM)
    smem = pl.BlockSpec(memory_space=pltpu.SMEM)
    own_index = pl.pallas_call(
        functools.partial(index_kernel, (n_ctx, rows, half, reach, key_pad)),
        out_shape=jax.ShapeDtypeStruct((rows, reach), jnp.float32),
        in_specs=[smem] + [vmem] * (3 + n_ctx),
        out_specs=vmem,
        scratch_shapes=[
            pltpu.VMEM((seq_len, idim), jnp.bfloat16),
            pltpu.VMEM((wide, idim), jnp.bfloat16),
            pltpu.SMEM((block_order.shape[0],), jnp.int32),
        ],
        name="index_scores",
    )(block_order, seg_table, index_query, index_weight.T, *pieces)

    group = 8
    steps = heads // group
    own_target = pl.pallas_call(
        functools.partial(target_kernel, (n_ctx, rows, half, reach, key_pad, key_width)),
        out_shape=jax.ShapeDtypeStruct((rows, reach), jnp.float32),
        grid=(steps,),
        in_specs=[
            smem,
            vmem,
            pl.BlockSpec((rows, group * key_width), lambda g: (0, g)),
        ]
        + [vmem] * n_ctx,
        out_specs=vmem,
        scratch_shapes=[
            pltpu.VMEM((seq_len, key_pad), jnp.bfloat16),
            pltpu.VMEM((rows // half, wide, key_pad), jnp.bfloat16),
            pltpu.VMEM((rows // half, wide, key_pad), jnp.bfloat16),
            pltpu.VMEM((rows // half, half, reach), jnp.float32),
            pltpu.SMEM((block_order.shape[0],), jnp.int32),
        ],
        name="target_sums",
    )(block_order, seg_table, main_query, *pieces)

    distances = [1 << k for k in range(n_head.bit_length() - 1)]
    sums = []
    for value in (own_target, own_index):
        for distance in distances[:-1]:
            value = value + swap(value, "head", distance)
        sums += [value, swap(value, "head", distances[-1])]
    loss = pl.pallas_call(
        functools.partial(loss_kernel, (rows, half, reach, heads * n_head)),
        out_shape=jax.ShapeDtypeStruct((1, rows), jnp.float32),
        in_specs=[smem] + [vmem] * 5,
        out_specs=vmem,
        name="row_losses",
    )(block_order, seg_table, *sums)
    return loss.reshape(rows)


def solution(mesh):
    in_specs = (
        P("ctx", None),
        P("ctx", None),
        P("ctx", "head"),
        P("ctx", "head"),
        P("ctx", "head"),
        P(),
        P(),
    )
    return jax.shard_map(
        per_device, mesh=mesh, in_specs=in_specs, out_specs=P("ctx"), check_vma=False
    )
```

```python
import functools
import math

import jax
import jax.numpy as jnp
from jax import lax
from jax.experimental import pallas as pl
from jax.experimental.pallas import tpu as pltpu
from jax.sharding import PartitionSpec as P

LANES = 128
score_scale = 192.0 ** (-0.5)
hidden = -1e30


def swap(x, axis, distance):
    size = lax.axis_size(axis)
    return lax.ppermute(x, axis, [(i, i ^ distance) for i in range(size)])


def window_masks(block, reach, half, seg_ref):
    table_rows = seg_ref.shape[0]
    first = block - reach // half
    row0 = lax.div(first + 2 * table_rows, 2) - table_rows
    pieces = []
    for k in range(reach // LANES + 2):
        row = jnp.clip(row0 + k, 0, table_rows - 1)
        pieces.append(seg_ref[pl.ds(row, 1), :].astype(jnp.float32))
    wide = jnp.concatenate(pieces, axis=1)
    width = wide.shape[1]
    moved = pltpu.roll(wide, width - half, 1)
    odd = lax.rem(first + 2 * table_rows, 2)
    wide = jnp.where(odd == 1, moved, wide)
    tail_seg = jnp.broadcast_to(wide[:, reach : reach + LANES], (half, LANES))
    head_seg = jnp.broadcast_to(wide[:, :LANES], (half, LANES))
    row_id = lax.broadcasted_iota(jnp.int32, (half, LANES), 0)
    lane_id = lax.broadcasted_iota(jnp.int32, (half, LANES), 1)
    query_seg = jnp.sum(jnp.where(row_id == lane_id, tail_seg, 0.0), axis=1, keepdims=True)
    in_tail = (lane_id <= row_id) & (lane_id < half)
    key_seg = jnp.concatenate(
        [jnp.where(in_tail, tail_seg, head_seg), jnp.broadcast_to(wide[:, LANES:reach], (half, reach - LANES))], axis=1
    )
    place = lax.broadcasted_iota(jnp.int32, (half, reach), 1)
    rows_full = lax.broadcasted_iota(jnp.int32, (half, reach), 0)
    tail_full = (place <= rows_full) & (place < half)
    position = first * half + place + jnp.where(tail_full, reach, 0)
    visible = (key_seg == query_seg) & (position >= 0)
    return in_tail, visible


def ring_fold(in_tail, wide, reach):
    low = jnp.where(in_tail, wide[:, reach : reach + LANES], wide[:, :LANES])
    return jnp.concatenate([low, wide[:, LANES:reach]], axis=1)


def own_block(keep):
    bit = lax.axis_index("head") & 1
    return bit if keep else 1 - bit


def setup_kernel(sizes, order_ref, seg_ref, weight_ref, bias_ref, gain_ref):
    half, reach = sizes
    me = lax.axis_index("ctx")
    for i in range(2):
        _, visible = window_masks(order_ref[me * 2 + i], reach, half, seg_ref)
        bias_ref[i] = jnp.where(visible, 0.0, hidden)
    gain_ref[...] = jnp.transpose(weight_ref[...].astype(jnp.float32), (1, 0))


def block_kernel(sizes, keep, order_ref, bias_ref, gain_ref, query_hbm, index_query_hbm, *refs):
    n_ctx, half, reach, key_width = sizes
    piece_refs = refs[:n_ctx]
    (out_ref, query_ref, index_query_ref, query_sem, index_sem,
     stack_ref, index_window, even_ref, odd_ref, inverse_ref) = refs[n_ctx:]
    wide = even_ref.shape[1]
    key_pad = even_ref.shape[0]
    idim = index_window.shape[1]
    me = lax.axis_index("ctx")
    mine = own_block(keep)
    rows_here = pl.ds(pl.multiple_of(mine * half, half), half)
    index_copy = pltpu.make_async_copy(index_query_hbm.at[rows_here, :], index_query_ref, index_sem)
    index_copy.start()
    query_copy = pltpu.make_async_copy(query_hbm.at[rows_here, :], query_ref, query_sem)
    query_copy.start()

    for s in range(n_ctx):
        stack_ref[me ^ s] = piece_refs[s][...]
    for slot in range(order_ref.shape[0]):
        inverse_ref[order_ref[slot]] = slot
    block = order_ref[me * 2 + mine]
    first = block - reach // half
    slots = [inverse_ref[jnp.maximum(first + w, 0)] for w in range(reach // half + 1)]

    for w, slot in enumerate(slots):
        at = pl.multiple_of(key_width + (slot & 1) * half, half)
        index_window[w * half : (w + 1) * half, :] = stack_ref[slot >> 1, pl.ds(at, half), :]
    index_window[reach + half :, :] = jnp.zeros((wide - reach - half, idim), index_window.dtype)
    left = lax.broadcasted_iota(jnp.int32, (key_width, LANES), 1) < half
    even_ref[key_width:, :] = jnp.zeros((key_pad - key_width, wide), even_ref.dtype)
    odd_ref[: key_pad - key_width, :] = jnp.zeros((key_pad - key_width, wide), odd_ref.dtype)
    for c in range(wide // LANES):
        halves = []
        for side in (0, 1):
            w = 2 * c + side
            if w >= len(slots):
                halves.append(halves[0])
                continue
            tile = stack_ref[slots[w] >> 1, :key_width, :].astype(jnp.float32)
            turned = pltpu.roll(tile, half, 1)
            halves.append(jnp.where((slots[w] & 1) == side, tile, turned))
        both = jnp.where(left, halves[0], halves[1]).astype(even_ref.dtype)
        even_ref[:key_width, c * LANES : (c + 1) * LANES] = both
        odd_ref[key_pad - key_width :, c * LANES : (c + 1) * LANES] = both

    row_id = lax.broadcasted_iota(jnp.int32, (half, LANES), 0)
    lane_id = lax.broadcasted_iota(jnp.int32, (half, LANES), 1)
    in_tail = (lane_id <= row_id) & (lane_id < half)
    bias = bias_ref[mine]
    gains = gain_ref[rows_here, :]
    index_heads = index_query_ref.shape[1] // idim
    index_copy.wait()
    lhs = jnp.concatenate([index_query_ref[:, j * idim : (j + 1) * idim] for j in range(index_heads)], axis=0)
    dots = lax.dot_general(lhs, index_window[...], (((1,), (1,)), ((), ())), preferred_element_type=jnp.float32)
    total = jnp.zeros((half, reach), jnp.float32)
    for j in range(index_heads):
        folded = ring_fold(in_tail, dots[j * half : (j + 1) * half, :], reach)
        total = total + gains[:, j : j + 1] * jnp.maximum(folded, 0.0)
    out_ref[1] = jnp.where(bias == 0.0, total, 0.0)

    heads = query_ref.shape[1] // key_width
    query_copy.wait()
    total = jnp.zeros((half, reach), jnp.float32)
    for parity, keys_ref in ((0, even_ref), (1, odd_ref)):
        starts = [g * 2 * key_width + parity * (2 * key_width - key_pad) for g in range(heads // 2)]
        lhs = jnp.concatenate([query_ref[:, at : at + key_pad] for at in starts], axis=0)
        raw = lax.dot_general(lhs, keys_ref[...], (((1,), (0,)), ((), ())), preferred_element_type=jnp.float32)
        for g in range(heads // 2):
            scores = ring_fold(in_tail, raw[g * half : (g + 1) * half, :], reach) + bias
            row_max = jnp.max(scores, axis=1, keepdims=True)
            powers = jnp.exp2((scores - row_max) * (score_scale * math.log2(math.e)))
            share = 1.0 / jnp.sum(powers, axis=1, keepdims=True)
            total = total + powers * share
    out_ref[0] = total


def loss_kernel(sizes, bias_ref, *refs):
    half, total_heads = sizes
    value_refs, out_ref = refs[:-1], refs[-1]
    mine = own_block(True)
    visible = bias_ref[mine] == 0.0
    target = functools.reduce(jnp.add, [ref[0] for ref in value_refs]) * (1.0 / total_heads)
    index_score = functools.reduce(jnp.add, [ref[1] for ref in value_refs])
    masked = jnp.where(visible, index_score, hidden)
    row_max = jnp.max(masked, axis=1, keepdims=True)
    exp_sum = jnp.sum(jnp.where(visible, jnp.exp(masked - row_max), 0.0), axis=1, keepdims=True)
    positive = target > 0.0
    logs = jnp.log(jnp.where(positive, target, 1.0))
    entropy_sum = jnp.sum(jnp.where(positive, target * logs, 0.0), axis=1, keepdims=True)
    cross_sum = jnp.sum(jnp.where(visible, target * index_score, 0.0), axis=1, keepdims=True)
    target_sum = jnp.sum(target, axis=1, keepdims=True)
    column = entropy_sum - cross_sum + (row_max + jnp.log(exp_sum)) * target_sum
    rows = out_ref.shape[1]
    row_id = lax.broadcasted_iota(jnp.int32, (half, rows), 0)
    lane_id = lax.broadcasted_iota(jnp.int32, (half, rows), 1)
    out_ref[...] = jnp.sum(jnp.where(row_id + mine * half == lane_id, column, 0.0), axis=0, keepdims=True)


def per_device(
    latent_keys, index_keys, main_query, index_query, index_weight, segment_ids, block_order
):
    n_ctx, n_head = lax.axis_size("ctx"), lax.axis_size("head")
    rows, key_width = latent_keys.shape
    idim = index_keys.shape[1]
    seq_len = segment_ids.shape[0]
    half = seq_len // block_order.shape[0]
    reach = seq_len // 4
    heads = main_query.shape[1] // key_width
    key_pad = -(-key_width // LANES) * LANES
    wide = reach + LANES

    packed = jnp.concatenate([latent_keys.T, index_keys], axis=0)
    own_core = [packed] + [swap(packed, "ctx", 2 * s) for s in range(1, n_ctx // 2)]
    pieces = []
    for piece in own_core:
        pieces += [piece, swap(piece, "ctx", 1)]
    seg_table = segment_ids.reshape(seq_len // LANES, LANES)

    vmem = pl.BlockSpec(memory_space=pltpu.VMEM)
    smem = pl.BlockSpec(memory_space=pltpu.SMEM)
    hbm = pl.BlockSpec(memory_space=pltpu.HBM)
    index_heads = index_weight.shape[1]
    bias, gains = pl.pallas_call(
        functools.partial(setup_kernel, (half, reach)),
        out_shape=(
            jax.ShapeDtypeStruct((2, half, reach), jnp.float32),
            jax.ShapeDtypeStruct((rows, index_heads), jnp.float32),
        ),
        in_specs=[smem, vmem, vmem],
        out_specs=(vmem, vmem),
        compiler_params=pltpu.CompilerParams(vmem_limit_bytes=8 << 20),
        cost_estimate=pl.CostEstimate(flops=1 << 20, bytes_accessed=1 << 20, transcendentals=0),
        name="masks",
    )(block_order, seg_table, index_weight.T)

    far_query = pltpu.with_memory_space_constraint(main_query, pltpu.HBM)
    far_index_query = pltpu.with_memory_space_constraint(index_query, pltpu.HBM)

    def block_sums(keep):
        return pl.pallas_call(
            functools.partial(block_kernel, (n_ctx, half, reach, key_width), keep),
            out_shape=jax.ShapeDtypeStruct((2, half, reach), jnp.float32),
            in_specs=[smem, vmem, vmem, hbm, hbm] + [vmem] * n_ctx,
            out_specs=vmem,
            scratch_shapes=[
                pltpu.VMEM((half, main_query.shape[1]), jnp.bfloat16),
                pltpu.VMEM((half, index_query.shape[1]), jnp.bfloat16),
                pltpu.SemaphoreType.DMA,
                pltpu.SemaphoreType.DMA,
                pltpu.VMEM((n_ctx, key_width + idim, LANES), jnp.bfloat16),
                pltpu.VMEM((wide, idim), jnp.bfloat16),
                pltpu.VMEM((key_pad, wide), jnp.bfloat16),
                pltpu.VMEM((key_pad, wide), jnp.bfloat16),
                pltpu.SMEM((block_order.shape[0],), jnp.int32),
            ],
            compiler_params=pltpu.CompilerParams(vmem_limit_bytes=28 << 20),
            cost_estimate=pl.CostEstimate(
                flops=2 * half * wide * (heads * key_pad + index_heads * idim), bytes_accessed=4 << 20, transcendentals=0
            ),
            name="keep_sums" if keep else "give_sums",
        )(block_order, bias, gains, far_query, far_index_query, *pieces)

    given = block_sums(False)
    kept = block_sums(True)
    value = kept + swap(given, "head", 1)
    distances = [1 << k for k in range(1, n_head.bit_length() - 1)]
    for distance in distances[:-1]:
        value = value + swap(value, "head", distance)
    values = [value] + [swap(value, "head", distance) for distance in distances[-1:]]
    loss = pl.pallas_call(
        functools.partial(loss_kernel, (half, heads * n_head)),
        out_shape=jax.ShapeDtypeStruct((1, rows), jnp.float32),
        in_specs=[vmem] * (1 + len(values)),
        out_specs=vmem,
        compiler_params=pltpu.CompilerParams(vmem_limit_bytes=8 << 20),
        name="row_losses",
    )(bias, *values)
    return (loss + swap(loss, "head", 1)).reshape(rows)


def solution(mesh):
    in_specs = (
        P("ctx", None),
        P("ctx", None),
        P("ctx", "head"),
        P("ctx", "head"),
        P("ctx", "head"),
        P(),
        P(),
    )
    return jax.shard_map(
        per_device, mesh=mesh, in_specs=in_specs, out_specs=P("ctx"), check_vma=False
    )
```

```python
import functools
import math

import jax
import jax.numpy as jnp
from jax import lax
from jax.experimental import pallas as pl
from jax.experimental.pallas import tpu as pltpu
from jax.sharding import PartitionSpec as P


LANES = 128
score_scale = 192.0 ** (-0.5)
hidden = -1e30


def swap(x, axis, distance):
    size = lax.axis_size(axis)
    return lax.ppermute(x, axis, [(i, i ^ distance) for i in range(size)])


def window_masks(block, reach, half, seg_ref):
    table_rows = seg_ref.shape[0]
    first = block - reach // half
    row0 = lax.div(first + 2 * table_rows, 2) - table_rows
    pieces = []
    for k in range(reach // LANES + 2):
        row = jnp.clip(row0 + k, 0, table_rows - 1)
        pieces.append(seg_ref[pl.ds(row, 1), :].astype(jnp.float32))
    wide = jnp.concatenate(pieces, axis=1)
    width = wide.shape[1]
    moved = pltpu.roll(wide, width - half, 1)
    odd = lax.rem(first + 2 * table_rows, 2)
    wide = jnp.where(odd == 1, moved, wide)
    tail_seg = jnp.broadcast_to(wide[:, reach : reach + LANES], (half, LANES))
    head_seg = jnp.broadcast_to(wide[:, :LANES], (half, LANES))
    row_id = lax.broadcasted_iota(jnp.int32, (half, LANES), 0)
    lane_id = lax.broadcasted_iota(jnp.int32, (half, LANES), 1)
    query_seg = jnp.sum(jnp.where(row_id == lane_id, tail_seg, 0.0), axis=1, keepdims=True)
    in_tail = (lane_id <= row_id) & (lane_id < half)
    key_seg = jnp.concatenate(
        [jnp.where(in_tail, tail_seg, head_seg), jnp.broadcast_to(wide[:, LANES:reach], (half, reach - LANES))], axis=1
    )
    place = lax.broadcasted_iota(jnp.int32, (half, reach), 1)
    rows_full = lax.broadcasted_iota(jnp.int32, (half, reach), 0)
    tail_full = (place <= rows_full) & (place < half)
    position = first * half + place + jnp.where(tail_full, reach, 0)
    visible = (key_seg == query_seg) & (position >= 0)
    return in_tail, visible


def ring_fold(in_tail, wide, reach):
    low = jnp.where(in_tail, wide[:, reach : reach + LANES], wide[:, :LANES])
    return jnp.concatenate([low, wide[:, LANES:reach]], axis=1)


def own_block(keep):
    bit = lax.axis_index("head") & 1
    return bit if keep else 1 - bit


def prelude_kernel(sizes, order_ref, seg_ref, weight_ref, query_hbm, index_query_hbm,
                   bias_ref, gain_ref, query_ref, index_query_ref, sems):
    half, reach, copies = sizes
    rows, _ = query_ref.shape
    waits = [pltpu.make_async_copy(index_query_hbm, index_query_ref, sems.at[copies])]
    for c in range(copies):
        part = slice(c * (rows // copies), (c + 1) * (rows // copies))
        waits.append(pltpu.make_async_copy(query_hbm.at[part, :], query_ref.at[part, :], sems.at[c]))
    for copy in waits:
        copy.start()
    me = lax.axis_index("ctx")
    for i in range(2):
        _, visible = window_masks(order_ref[me * 2 + i], reach, half, seg_ref)
        bias_ref[i] = jnp.where(visible, 0.0, hidden)
    gain_ref[...] = jnp.transpose(weight_ref[...].astype(jnp.float32), (1, 0))
    for copy in waits:
        copy.wait()


def block_kernel(sizes, keep, order_ref, bias_ref, gain_ref, query_ref, index_query_ref, *refs):
    n_ctx, half, reach, key_width = sizes
    piece_refs = refs[:n_ctx]
    out_ref, stack_ref, index_window, even_ref, odd_ref, inverse_ref = refs[n_ctx:]
    wide = even_ref.shape[1]
    key_pad = even_ref.shape[0]
    idim = index_window.shape[1]
    me = lax.axis_index("ctx")
    mine = own_block(keep)
    rows_here = pl.ds(pl.multiple_of(mine * half, half), half)
    for s in range(n_ctx):
        stack_ref[me ^ s] = piece_refs[s][...]
    for slot in range(order_ref.shape[0]):
        inverse_ref[order_ref[slot]] = slot
    block = order_ref[me * 2 + mine]
    first = block - reach // half
    slots = [inverse_ref[jnp.maximum(first + w, 0)] for w in range(reach // half + 1)]

    for w, slot in enumerate(slots):
        at = pl.multiple_of(key_width + (slot & 1) * half, half)
        index_window[w * half : (w + 1) * half, :] = stack_ref[slot >> 1, pl.ds(at, half), :]
    index_window[reach + half :, :] = jnp.zeros((wide - reach - half, idim), index_window.dtype)
    left = lax.broadcasted_iota(jnp.int32, (key_width, LANES), 1) < half
    even_ref[key_width:, :] = jnp.zeros((key_pad - key_width, wide), even_ref.dtype)
    odd_ref[: key_pad - key_width, :] = jnp.zeros((key_pad - key_width, wide), odd_ref.dtype)
    for c in range(wide // LANES):
        halves = []
        for side in (0, 1):
            w = 2 * c + side
            if w >= len(slots):
                halves.append(halves[0])
                continue
            tile = stack_ref[slots[w] >> 1, :key_width, :].astype(jnp.float32)
            turned = pltpu.roll(tile, half, 1)
            halves.append(jnp.where((slots[w] & 1) == side, tile, turned))
        both = jnp.where(left, halves[0], halves[1]).astype(even_ref.dtype)
        even_ref[:key_width, c * LANES : (c + 1) * LANES] = both
        odd_ref[key_pad - key_width :, c * LANES : (c + 1) * LANES] = both

    row_id = lax.broadcasted_iota(jnp.int32, (half, LANES), 0)
    lane_id = lax.broadcasted_iota(jnp.int32, (half, LANES), 1)
    in_tail = (lane_id <= row_id) & (lane_id < half)
    bias = bias_ref[mine]
    gains = gain_ref[rows_here, :]
    index_heads = index_query_ref.shape[1] // idim
    lhs = jnp.concatenate([index_query_ref[rows_here, j * idim : (j + 1) * idim] for j in range(index_heads)], axis=0)
    dots = lax.dot_general(lhs, index_window[...], (((1,), (1,)), ((), ())), preferred_element_type=jnp.float32)
    total = jnp.zeros((half, reach), jnp.float32)
    for j in range(index_heads):
        folded = ring_fold(in_tail, dots[j * half : (j + 1) * half, :], reach)
        total = total + gains[:, j : j + 1] * jnp.maximum(folded, 0.0)
    out_ref[1] = jnp.where(bias == 0.0, total, 0.0)

    heads = query_ref.shape[1] // key_width
    total = jnp.zeros((half, reach), jnp.float32)
    for parity, keys_ref in ((0, even_ref), (1, odd_ref)):
        starts = [g * 2 * key_width + parity * (2 * key_width - key_pad) for g in range(heads // 2)]
        lhs = jnp.concatenate([query_ref[rows_here, at : at + key_pad] for at in starts], axis=0)
        raw = lax.dot_general(lhs, keys_ref[...], (((1,), (0,)), ((), ())), preferred_element_type=jnp.float32)
        for g in range(heads // 2):
            scores = ring_fold(in_tail, raw[g * half : (g + 1) * half, :], reach) + bias
            row_max = jnp.max(scores, axis=1, keepdims=True)
            powers = jnp.exp2((scores - row_max) * (score_scale * math.log2(math.e)))
            share = 1.0 / jnp.sum(powers, axis=1, keepdims=True)
            total = total + powers * share
    out_ref[0] = total


def loss_kernel(sizes, bias_ref, *refs):
    half, total_heads = sizes
    value_refs, out_ref = refs[:-1], refs[-1]
    mine = own_block(True)
    visible = bias_ref[mine] == 0.0
    target = functools.reduce(jnp.add, [ref[0] for ref in value_refs]) * (1.0 / total_heads)
    index_score = functools.reduce(jnp.add, [ref[1] for ref in value_refs])
    masked = jnp.where(visible, index_score, hidden)
    row_max = jnp.max(masked, axis=1, keepdims=True)
    exp_sum = jnp.sum(jnp.where(visible, jnp.exp(masked - row_max), 0.0), axis=1, keepdims=True)
    positive = target > 0.0
    logs = jnp.log(jnp.where(positive, target, 1.0))
    entropy_sum = jnp.sum(jnp.where(positive, target * logs, 0.0), axis=1, keepdims=True)
    cross_sum = jnp.sum(jnp.where(visible, target * index_score, 0.0), axis=1, keepdims=True)
    target_sum = jnp.sum(target, axis=1, keepdims=True)
    column = entropy_sum - cross_sum + (row_max + jnp.log(exp_sum)) * target_sum
    rows = out_ref.shape[1]
    row_id = lax.broadcasted_iota(jnp.int32, (half, rows), 0)
    lane_id = lax.broadcasted_iota(jnp.int32, (half, rows), 1)
    out_ref[...] = jnp.sum(jnp.where(row_id + mine * half == lane_id, column, 0.0), axis=0, keepdims=True)


def per_device(
    latent_keys, index_keys, main_query, index_query, index_weight, segment_ids, block_order
):
    n_ctx, n_head = lax.axis_size("ctx"), lax.axis_size("head")
    rows, key_width = latent_keys.shape
    idim = index_keys.shape[1]
    seq_len = segment_ids.shape[0]
    half = seq_len // block_order.shape[0]
    reach = seq_len // 4
    heads = main_query.shape[1] // key_width
    key_pad = -(-key_width // LANES) * LANES
    wide = reach + LANES

    vmem = pl.BlockSpec(memory_space=pltpu.VMEM)
    smem = pl.BlockSpec(memory_space=pltpu.SMEM)
    hbm = pl.BlockSpec(memory_space=pltpu.HBM)
    index_heads = index_weight.shape[1]

    packed = jnp.concatenate([latent_keys.T, index_keys], axis=0)
    own_core = [packed]
    for s in reversed(range(1, n_ctx // 2)):
        own_core.append(swap(packed, "ctx", 2 * s))
    own_core = [packed] + own_core[:0:-1]
    pieces = []
    for piece in own_core:
        pieces += [piece, swap(piece, "ctx", 1)]
    seg_table = segment_ids.reshape(seq_len // LANES, LANES)

    copies = 8
    far_query = pltpu.with_memory_space_constraint(main_query, pltpu.HBM)
    far_index_query = pltpu.with_memory_space_constraint(index_query, pltpu.HBM)
    bias, gains, near_query, near_index_query = pl.pallas_call(
        functools.partial(prelude_kernel, (half, reach, copies)),
        out_shape=(
            jax.ShapeDtypeStruct((2, half, reach), jnp.float32),
            jax.ShapeDtypeStruct((rows, index_heads), jnp.float32),
            jax.ShapeDtypeStruct(main_query.shape, main_query.dtype),
            jax.ShapeDtypeStruct(index_query.shape, index_query.dtype),
        ),
        in_specs=[smem, vmem, vmem, hbm, hbm],
        out_specs=(vmem, vmem, vmem, vmem),
        scratch_shapes=[pltpu.SemaphoreType.DMA((copies + 1,))],
        compiler_params=pltpu.CompilerParams(vmem_limit_bytes=12 << 20),
        cost_estimate=pl.CostEstimate(flops=1 << 20, bytes_accessed=10 << 20, transcendentals=0),
        name="prelude",
    )(block_order, seg_table, index_weight.T, far_query, far_index_query)

    def block_sums(keep):
        return pl.pallas_call(
            functools.partial(block_kernel, (n_ctx, half, reach, key_width), keep),
            out_shape=jax.ShapeDtypeStruct((2, half, reach), jnp.float32),
            in_specs=[smem] + [vmem] * (4 + n_ctx),
            out_specs=vmem,
            scratch_shapes=[
                pltpu.VMEM((n_ctx, key_width + idim, LANES), jnp.bfloat16),
                pltpu.VMEM((wide, idim), jnp.bfloat16),
                pltpu.VMEM((key_pad, wide), jnp.bfloat16),
                pltpu.VMEM((key_pad, wide), jnp.bfloat16),
                pltpu.SMEM((block_order.shape[0],), jnp.int32),
            ],
            compiler_params=pltpu.CompilerParams(vmem_limit_bytes=28 << 20),
            cost_estimate=pl.CostEstimate(
                flops=2 * half * wide * (heads * key_pad + index_heads * idim), bytes_accessed=4 << 20, transcendentals=0
            ),
            name="keep_sums" if keep else "give_sums",
        )(block_order, bias, gains, near_query, near_index_query, *pieces)

    given = block_sums(False)
    kept = block_sums(True)
    value = kept + swap(given, "head", 1)
    distances = [1 << k for k in range(1, n_head.bit_length() - 1)]
    for distance in distances[:-1]:
        value = value + swap(value, "head", distance)
    values = [value] + [swap(value, "head", distance) for distance in distances[-1:]]
    loss = pl.pallas_call(
        functools.partial(loss_kernel, (half, heads * n_head)),
        out_shape=jax.ShapeDtypeStruct((1, rows), jnp.float32),
        in_specs=[vmem] * (1 + len(values)),
        out_specs=vmem,
        compiler_params=pltpu.CompilerParams(vmem_limit_bytes=8 << 20),
        name="row_losses",
    )(bias, *values)
    return (loss + swap(loss, "head", 1)).reshape(rows)


def solution(mesh):
    in_specs = (
        P("ctx", None),
        P("ctx", None),
        P("ctx", "head"),
        P("ctx", "head"),
        P("ctx", "head"),
        P(),
        P(),
    )
    return jax.shard_map(per_device, mesh=mesh, in_specs=in_specs, out_specs=P("ctx"), check_vma=False)
```

```python
import functools
import math

import jax
import jax.numpy as jnp
from jax import lax
from jax.experimental import pallas as pl
from jax.experimental.pallas import tpu as pltpu
from jax.sharding import PartitionSpec as P


LANES = 128
score_scale = 192.0 ** (-0.5)
hidden = -1e30


def swap(x, axis, distance):
    size = lax.axis_size(axis)
    return lax.ppermute(x, axis, [(i, i ^ distance) for i in range(size)])


def window_masks(block, reach, half, seg_ref):
    table_rows = seg_ref.shape[0]
    first = block - reach // half
    row0 = lax.div(first + 2 * table_rows, 2) - table_rows
    pieces = []
    for k in range(reach // LANES + 2):
        row = jnp.clip(row0 + k, 0, table_rows - 1)
        pieces.append(seg_ref[pl.ds(row, 1), :].astype(jnp.float32))
    wide = jnp.concatenate(pieces, axis=1)
    width = wide.shape[1]
    moved = pltpu.roll(wide, width - half, 1)
    odd = lax.rem(first + 2 * table_rows, 2)
    wide = jnp.where(odd == 1, moved, wide)
    tail_seg = jnp.broadcast_to(wide[:, reach : reach + LANES], (half, LANES))
    head_seg = jnp.broadcast_to(wide[:, :LANES], (half, LANES))
    row_id = lax.broadcasted_iota(jnp.int32, (half, LANES), 0)
    lane_id = lax.broadcasted_iota(jnp.int32, (half, LANES), 1)
    query_seg = jnp.sum(jnp.where(row_id == lane_id, tail_seg, 0.0), axis=1, keepdims=True)
    in_tail = (lane_id <= row_id) & (lane_id < half)
    key_seg = jnp.concatenate(
        [jnp.where(in_tail, tail_seg, head_seg), jnp.broadcast_to(wide[:, LANES:reach], (half, reach - LANES))], axis=1
    )
    place = lax.broadcasted_iota(jnp.int32, (half, reach), 1)
    rows_full = lax.broadcasted_iota(jnp.int32, (half, reach), 0)
    tail_full = (place <= rows_full) & (place < half)
    position = first * half + place + jnp.where(tail_full, reach, 0)
    visible = (key_seg == query_seg) & (position >= 0)
    return in_tail, visible


def ring_fold(own_low, main, tail):
    low = jnp.where(own_low, main[:, :LANES], tail)
    return jnp.concatenate([low, main[:, LANES:]], axis=1)


def own_block(keep):
    bit = lax.axis_index("head") & 1
    return bit if keep else 1 - bit


def block_rows(keep, half):
    return pl.ds(pl.multiple_of(own_block(keep) * half, half), half)


def pack_kernel(latent_hbm, index_hbm, out_ref, sems):
    width = latent_hbm.shape[0]
    copies = [
        pltpu.make_async_copy(latent_hbm, out_ref.at[:width, :], sems.at[0]),
        pltpu.make_async_copy(index_hbm, out_ref.at[width:, :], sems.at[1]),
    ]
    for copy in copies:
        copy.start()
    for copy in copies:
        copy.wait()


def prelude_kernel(sizes, order_hbm, seg_hbm, weight_hbm, query_hbm, index_query_hbm,
                   bias_ref, query_ref, keep_ref, give_ref, order_ref, seg_ref, weight_ref, sems):
    half, reach, copies = sizes
    rows = query_ref.shape[0]
    width = index_query_hbm.shape[1]
    small = [
        pltpu.make_async_copy(order_hbm, order_ref, sems.at[0]),
        pltpu.make_async_copy(seg_hbm, seg_ref, sems.at[1]),
        pltpu.make_async_copy(weight_hbm, weight_ref, sems.at[2]),
    ]
    large = [
        pltpu.make_async_copy(index_query_hbm.at[block_rows(False, half), :], give_ref.at[:, :width], sems.at[3]),
        pltpu.make_async_copy(index_query_hbm.at[block_rows(True, half), :], keep_ref.at[:, :width], sems.at[4]),
    ]
    for c in range(copies):
        part = slice(c * (rows // copies), (c + 1) * (rows // copies))
        large.append(pltpu.make_async_copy(query_hbm.at[part, :], query_ref.at[part, :], sems.at[5 + c]))
    for copy in small + large:
        copy.start()
    for copy in small:
        copy.wait()
    me = lax.axis_index("ctx")
    for i in range(2):
        _, visible = window_masks(order_ref[me * 2 + i], reach, half, seg_ref)
        bias_ref[i] = jnp.where(visible, 0.0, hidden)
    gains = jnp.transpose(weight_ref[...].astype(jnp.float32), (1, 0))
    gains = jnp.concatenate([gains, jnp.zeros((rows, LANES - gains.shape[1]), gains.dtype)], axis=1)
    gains = gains.astype(keep_ref.dtype)
    first_kept = own_block(True) == 0
    keep_ref[:, width:] = jnp.where(first_kept, gains[:half], gains[half:])
    give_ref[:, width:] = jnp.where(first_kept, gains[half:], gains[:half])
    for copy in large:
        copy.wait()


def block_kernel(sizes, keep, order_ref, seg_ref, bias_ref, query_ref, *refs):
    n_ctx, half, reach, key_width, idim = sizes
    n_index = 2 if keep else 0
    index_query_refs, refs = refs[:n_index], refs[n_index:]
    piece_refs, out_refs = refs[:n_ctx], refs[n_ctx : n_ctx + 1 + (n_index > 0)]
    refs = refs[n_ctx + len(out_refs) :]
    stack_ref, main_ref, tail_ref, index_main, index_tail, raw_ref, index_raw, inverse_ref = refs
    key_pad = main_ref.shape[1]
    me = lax.axis_index("ctx")
    mine = own_block(keep)
    rows_here = block_rows(keep, half)
    for s in range(n_ctx):
        stack_ref[me ^ s] = piece_refs[s][...]
    for slot in range(order_ref.shape[0]):
        inverse_ref[order_ref[slot]] = slot
    block = order_ref[me * 2 + mine]
    reach_blocks = reach // half
    first = block - reach_blocks
    oldest = jnp.maximum(first, 0) * half + half - 1
    needed = (first >= 0) & (seg_ref[block * half] == seg_ref[oldest])
    order = [reach_blocks] + list(range(1, reach_blocks)) + [0]
    slots = [inverse_ref[jnp.maximum(first + w, 0)] for w in order]

    left = lax.broadcasted_iota(jnp.int32, (key_width, LANES), 1) < half

    def keys_into(target_ref, c, lanes):
        halves = []
        for side in (0, 1):
            slot = slots[min(2 * c + side, reach_blocks)]
            tile = stack_ref[slot >> 1, :key_width, :].astype(jnp.float32)
            turned = pltpu.roll(tile, half, 1)
            halves.append(jnp.where((slot & 1) == side, tile, turned))
        both = jnp.where(left, halves[0], halves[1]).astype(target_ref.dtype)
        target_ref[0, :key_width, lanes] = both
        target_ref[1, key_pad - key_width :, lanes] = both

    def index_keys_into(target_ref, w, at):
        start = pl.multiple_of(key_width + (slots[w] & 1) * half, half)
        target_ref[at : at + half, :] = stack_ref[slots[w] >> 1, pl.ds(start, half), :]

    main_ref[0, key_width:, :] = jnp.zeros((key_pad - key_width, reach), main_ref.dtype)
    main_ref[1, : key_pad - key_width, :] = jnp.zeros((key_pad - key_width, reach), main_ref.dtype)
    for c in range(reach // LANES):
        keys_into(main_ref, c, slice(c * LANES, (c + 1) * LANES))

    row_id = lax.broadcasted_iota(jnp.int32, (half, LANES), 0)
    lane_id = lax.broadcasted_iota(jnp.int32, (half, LANES), 1)
    own_low = (lane_id <= row_id) | (lane_id >= half) | jnp.logical_not(needed)
    bias = bias_ref[mine]

    heads = query_ref.shape[1] // key_width
    stacked_queries = []
    for parity in (0, 1):
        starts = [g * 2 * key_width + parity * (2 * key_width - key_pad) for g in range(heads // 2)]
        stacked_queries.append(lambda starts=starts: jnp.concatenate([query_ref[rows_here, at : at + key_pad] for at in starts], axis=0))

    def index_lhs(ref):
        return jnp.concatenate([ref[:, j * idim : (j + 1) * idim] for j in range(ref.shape[1] // idim - 1)], axis=0)

    if keep:
        for w in range(reach_blocks):
            index_keys_into(index_main, w, w * half)

    @pl.when(needed)
    def _():
        tail_ref[0, key_width:, :] = jnp.zeros((key_pad - key_width, LANES), tail_ref.dtype)
        tail_ref[1, : key_pad - key_width, :] = jnp.zeros((key_pad - key_width, LANES), tail_ref.dtype)
        keys_into(tail_ref, reach // LANES, slice(0, LANES))
        for parity in (0, 1):
            raw_ref[parity] = lax.dot_general(
                stacked_queries[parity](), tail_ref[parity], (((1,), (0,)), ((), ())), preferred_element_type=jnp.float32
            )
        if keep:
            index_keys_into(index_tail, reach_blocks, 0)
            index_tail[half:, :] = jnp.zeros((LANES - half, idim), index_tail.dtype)
            for k, ref in enumerate(index_query_refs):
                index_raw[k] = lax.dot_general(
                    index_lhs(ref), index_tail[...], (((1,), (1,)), ((), ())), preferred_element_type=jnp.float32
                )

    total = jnp.zeros((half, reach), jnp.float32)
    for parity in (0, 1):
        raw = lax.dot_general(
            stacked_queries[parity](), main_ref[parity], (((1,), (0,)), ((), ())), preferred_element_type=jnp.float32
        )
        for g in range(heads // 2):
            here = slice(g * half, (g + 1) * half)
            scores = ring_fold(own_low, raw[here, :], raw_ref[parity, here, :]) + bias
            row_max = jnp.max(scores, axis=1, keepdims=True)
            powers = jnp.exp2((scores - row_max) * (score_scale * math.log2(math.e)))
            share = 1.0 / jnp.sum(powers, axis=1, keepdims=True)
            total = total + powers * share
    out_refs[0][...] = total

    if keep:
        total = jnp.zeros((half, reach), jnp.float32)
        for k, ref in enumerate(index_query_refs):
            lhs = index_lhs(ref)
            dots = lax.dot_general(lhs, index_main[...], (((1,), (1,)), ((), ())), preferred_element_type=jnp.float32)
            gains = ref[:, lhs.shape[0] // half * idim :].astype(jnp.float32)
            for j in range(lhs.shape[0] // half):
                here = slice(j * half, (j + 1) * half)
                folded = ring_fold(own_low, dots[here, :], index_raw[k, here, :])
                total = total + gains[:, j : j + 1] * jnp.maximum(folded, 0.0)
        out_refs[1][...] = jnp.where(bias == 0.0, total, 0.0)


def loss_kernel(sizes, bias_ref, *refs):
    half, total_heads = sizes
    value_refs, out_ref = refs[:-1], refs[-1]
    mine = own_block(True)
    visible = bias_ref[mine] == 0.0
    target = functools.reduce(jnp.add, [ref[0] for ref in value_refs]) * (1.0 / total_heads)
    index_score = functools.reduce(jnp.add, [ref[1] for ref in value_refs])
    masked = jnp.where(visible, index_score, hidden)
    row_max = jnp.max(masked, axis=1, keepdims=True)
    exp_sum = jnp.sum(jnp.where(visible, jnp.exp(masked - row_max), 0.0), axis=1, keepdims=True)
    positive = target > 0.0
    logs = jnp.log(jnp.where(positive, target, 1.0))
    entropy_sum = jnp.sum(jnp.where(positive, target * logs, 0.0), axis=1, keepdims=True)
    cross_sum = jnp.sum(jnp.where(visible, target * index_score, 0.0), axis=1, keepdims=True)
    target_sum = jnp.sum(target, axis=1, keepdims=True)
    column = entropy_sum - cross_sum + (row_max + jnp.log(exp_sum)) * target_sum
    rows = out_ref.shape[1]
    row_id = lax.broadcasted_iota(jnp.int32, (half, rows), 0)
    lane_id = lax.broadcasted_iota(jnp.int32, (half, rows), 1)
    out_ref[...] = jnp.sum(jnp.where(row_id + mine * half == lane_id, column, 0.0), axis=0, keepdims=True)


def per_device(
    latent_keys, index_keys, main_query, index_query, index_weight, segment_ids, block_order
):
    n_ctx, n_head = lax.axis_size("ctx"), lax.axis_size("head")
    rows, key_width = latent_keys.shape
    idim = index_keys.shape[1]
    seq_len = segment_ids.shape[0]
    half = seq_len // block_order.shape[0]
    reach = seq_len // 4
    heads = main_query.shape[1] // key_width
    key_pad = -(-key_width // LANES) * LANES
    vmem = pl.BlockSpec(memory_space=pltpu.VMEM)
    smem = pl.BlockSpec(memory_space=pltpu.SMEM)
    hbm = pl.BlockSpec(memory_space=pltpu.HBM)
    index_heads = index_weight.shape[1]

    def far(x):
        return pltpu.with_memory_space_constraint(x, pltpu.HBM)

    packed = pl.pallas_call(
        pack_kernel,
        out_shape=jax.ShapeDtypeStruct((key_width + idim, rows), latent_keys.dtype),
        in_specs=[hbm, hbm],
        out_specs=vmem,
        scratch_shapes=[pltpu.SemaphoreType.DMA((2,))],
        compiler_params=pltpu.CompilerParams(vmem_limit_bytes=2 << 20),
        name="pack",
    )(far(latent_keys.T), far(index_keys))
    own_core = [packed]
    for s in reversed(range(1, n_ctx // 2)):
        own_core.append(swap(packed, "ctx", 2 * s))
    own_core = [packed] + own_core[:0:-1]
    pieces = []
    for piece in own_core:
        pieces += [piece, swap(piece, "ctx", 1)]
    seg_table = segment_ids.reshape(seq_len // LANES, LANES)

    copies = 8
    index_row = (half, index_query.shape[1] + LANES)
    bias, near_query, keep_query, give_query = pl.pallas_call(
        functools.partial(prelude_kernel, (half, reach, copies)),
        out_shape=(
            jax.ShapeDtypeStruct((2, half, reach), jnp.float32),
            jax.ShapeDtypeStruct(main_query.shape, main_query.dtype),
            jax.ShapeDtypeStruct(index_row, index_query.dtype),
            jax.ShapeDtypeStruct(index_row, index_query.dtype),
        ),
        in_specs=[hbm] * 5,
        out_specs=(vmem,) * 4,
        scratch_shapes=[
            pltpu.SMEM(block_order.shape, jnp.int32),
            pltpu.VMEM(seg_table.shape, jnp.int32),
            pltpu.VMEM((index_heads, rows), index_weight.dtype),
            pltpu.SemaphoreType.DMA((copies + 5,)),
        ],
        compiler_params=pltpu.CompilerParams(vmem_limit_bytes=12 << 20),
        cost_estimate=pl.CostEstimate(flops=1 << 20, bytes_accessed=10 << 20, transcendentals=0),
        name="prelude",
    )(far(block_order), far(seg_table), far(index_weight.T), far(main_query), far(index_query))
    taken_query = swap(give_query, "head", 1)

    def block_sums(keep):
        sums = jax.ShapeDtypeStruct((half, reach), jnp.float32)
        index_queries = [keep_query, taken_query] if keep else []
        return pl.pallas_call(
            functools.partial(block_kernel, (n_ctx, half, reach, key_width, idim), keep),
            out_shape=(sums, sums) if keep else (sums,),
            in_specs=[smem, smem] + [vmem] * (2 + len(index_queries) + n_ctx),
            out_specs=(vmem, vmem) if keep else (vmem,),
            scratch_shapes=[
                pltpu.VMEM((n_ctx, key_width + idim, LANES), jnp.bfloat16),
                pltpu.VMEM((2, key_pad, reach), jnp.bfloat16),
                pltpu.VMEM((2, key_pad, LANES), jnp.bfloat16),
                pltpu.VMEM((reach, idim), jnp.bfloat16),
                pltpu.VMEM((LANES, idim), jnp.bfloat16),
                pltpu.VMEM((2, heads // 2 * half, LANES), jnp.float32),
                pltpu.VMEM((2, index_heads * half, LANES), jnp.float32),
                pltpu.SMEM((block_order.shape[0],), jnp.int32),
            ],
            compiler_params=pltpu.CompilerParams(vmem_limit_bytes=28 << 20),
            cost_estimate=pl.CostEstimate(
                flops=2 * half * reach * heads * key_pad, bytes_accessed=4 << 20, transcendentals=0
            ),
            name="keep_sums" if keep else "give_sums",
        )(block_order, segment_ids, bias, near_query, *index_queries, *pieces)

    given = block_sums(False)[0]
    kept, index_sums = block_sums(True)
    value = jnp.stack([kept + swap(given, "head", 1), index_sums])
    distances = [1 << k for k in range(1, n_head.bit_length() - 1)]
    for distance in distances[:-1]:
        value = value + swap(value, "head", distance)
    values = [value] + [swap(value, "head", distance) for distance in distances[-1:]]
    loss = pl.pallas_call(
        functools.partial(loss_kernel, (half, heads * n_head)),
        out_shape=jax.ShapeDtypeStruct((1, rows), jnp.float32),
        in_specs=[vmem] * (1 + len(values)),
        out_specs=vmem,
        compiler_params=pltpu.CompilerParams(vmem_limit_bytes=8 << 20),
        name="row_losses",
    )(bias, *values)
    return (loss + swap(loss, "head", 1)).reshape(rows)


def solution(mesh):
    in_specs = (
        P("ctx", None),
        P("ctx", None),
        P("ctx", "head"),
        P("ctx", "head"),
        P("ctx", "head"),
        P(),
        P(),
    )
    return jax.shard_map(per_device, mesh=mesh, in_specs=in_specs, out_specs=P("ctx"), check_vma=False)
```

```python
import functools
import math

import jax
import jax.numpy as jnp
from jax import lax
from jax.experimental import pallas as pl
from jax.experimental.pallas import tpu as pltpu
from jax.sharding import PartitionSpec as P


LANES = 128
score_scale = 192.0 ** (-0.5)
hidden = -1e30


def swap(x, axis, distance):
    size = lax.axis_size(axis)
    return lax.ppermute(x, axis, [(i, i ^ distance) for i in range(size)])


def window_masks(block, reach, half, seg_ref):
    table_rows = seg_ref.shape[0]
    first = block - reach // half
    row0 = lax.div(first + 2 * table_rows, 2) - table_rows
    pieces = []
    for k in range(reach // LANES + 2):
        row = jnp.clip(row0 + k, 0, table_rows - 1)
        pieces.append(seg_ref[pl.ds(row, 1), :].astype(jnp.float32))
    wide = jnp.concatenate(pieces, axis=1)
    width = wide.shape[1]
    moved = pltpu.roll(wide, width - half, 1)
    odd = lax.rem(first + 2 * table_rows, 2)
    wide = jnp.where(odd == 1, moved, wide)
    tail_seg = jnp.broadcast_to(wide[:, reach : reach + LANES], (half, LANES))
    head_seg = jnp.broadcast_to(wide[:, :LANES], (half, LANES))
    row_id = lax.broadcasted_iota(jnp.int32, (half, LANES), 0)
    lane_id = lax.broadcasted_iota(jnp.int32, (half, LANES), 1)
    query_seg = jnp.sum(jnp.where(row_id == lane_id, tail_seg, 0.0), axis=1, keepdims=True)
    in_tail = (lane_id <= row_id) & (lane_id < half)
    key_seg = jnp.concatenate(
        [jnp.where(in_tail, tail_seg, head_seg), jnp.broadcast_to(wide[:, LANES:reach], (half, reach - LANES))], axis=1
    )
    place = lax.broadcasted_iota(jnp.int32, (half, reach), 1)
    rows_full = lax.broadcasted_iota(jnp.int32, (half, reach), 0)
    tail_full = (place <= rows_full) & (place < half)
    position = first * half + place + jnp.where(tail_full, reach, 0)
    visible = (key_seg == query_seg) & (position >= 0)
    return in_tail, visible


def ring_fold(own_low, main, tail):
    low = jnp.where(own_low, main[:, :LANES], tail)
    return jnp.concatenate([low, main[:, LANES:]], axis=1)


def own_block(keep):
    bit = lax.axis_index("head") & 1
    return bit if keep else 1 - bit


def block_rows(keep, half):
    return pl.ds(pl.multiple_of(own_block(keep) * half, half), half)


def pack_kernel(latent_hbm, index_hbm, out_ref, part_ref, sems):
    width = latent_hbm.shape[0]
    part = part_ref.shape[0]
    bit = own_block(True)
    whole = [
        pltpu.make_async_copy(latent_hbm, out_ref.at[:width, :], sems.at[0]),
        pltpu.make_async_copy(index_hbm, out_ref.at[width:, :], sems.at[1]),
    ]
    low = [pltpu.make_async_copy(latent_hbm.at[:part, :], part_ref, sems.at[2])]
    high = [
        pltpu.make_async_copy(latent_hbm.at[part:, :], part_ref.at[: width - part, :], sems.at[2]),
        pltpu.make_async_copy(index_hbm, part_ref.at[width - part :, :], sems.at[3]),
    ]

    def each(copies, act):
        for copy in copies:
            act(copy)

    for act in (lambda copy: copy.start(), lambda copy: copy.wait()):
        each(whole, act)
        pl.when(bit == 0)(functools.partial(each, low, act))
        pl.when(bit == 1)(functools.partial(each, high, act))


def prelude_kernel(sizes, order_hbm, seg_hbm, weight_hbm, query_hbm, index_query_hbm,
                   bias_ref, query_ref, keep_ref, give_ref, order_ref, seg_ref, weight_ref, sems):
    half, reach, copies = sizes
    rows = query_ref.shape[0]
    width = index_query_hbm.shape[1]
    small = [
        pltpu.make_async_copy(order_hbm, order_ref, sems.at[0]),
        pltpu.make_async_copy(seg_hbm, seg_ref, sems.at[1]),
        pltpu.make_async_copy(weight_hbm, weight_ref, sems.at[2]),
    ]
    large = [
        pltpu.make_async_copy(index_query_hbm.at[block_rows(False, half), :], give_ref.at[:, :width], sems.at[3]),
        pltpu.make_async_copy(index_query_hbm.at[block_rows(True, half), :], keep_ref.at[:, :width], sems.at[4]),
    ]
    for c in range(copies):
        part = slice(c * (rows // copies), (c + 1) * (rows // copies))
        large.append(pltpu.make_async_copy(query_hbm.at[part, :], query_ref.at[part, :], sems.at[5 + c]))
    for copy in small + large:
        copy.start()
    for copy in small:
        copy.wait()
    me = lax.axis_index("ctx")
    for i in range(2):
        _, visible = window_masks(order_ref[me * 2 + i], reach, half, seg_ref)
        bias_ref[i] = jnp.where(visible, 0.0, hidden)
    gains = jnp.transpose(weight_ref[...].astype(jnp.float32), (1, 0))
    gains = jnp.concatenate([gains, jnp.zeros((rows, LANES - gains.shape[1]), gains.dtype)], axis=1)
    gains = gains.astype(keep_ref.dtype)
    first_kept = own_block(True) == 0
    keep_ref[:, width:] = jnp.where(first_kept, gains[:half], gains[half:])
    give_ref[:, width:] = jnp.where(first_kept, gains[half:], gains[:half])
    for copy in large:
        copy.wait()


def block_kernel(sizes, keep, order_ref, seg_ref, bias_ref, query_ref, *refs):
    n_ctx, half, reach, key_width, idim = sizes
    n_index = 2 if keep else 0
    index_query_refs, refs = refs[:n_index], refs[n_index:]
    if keep:
        stack_ref, refs = refs[0], refs[1:]
    else:
        piece_refs, half_refs, refs = refs[: n_ctx - 2], refs[n_ctx - 2 : n_ctx + 2], refs[n_ctx + 2 :]
    out_refs, refs = refs[:2], refs[2:]
    main_ref, tail_ref, index_main, index_tail, raw_ref, index_raw, main_raw, inverse_ref = refs
    key_pad = main_ref.shape[1]
    me = lax.axis_index("ctx")
    mine = own_block(keep)
    rows_here = block_rows(keep, half)
    if not keep:
        stack_ref = out_refs[1]
        bit = own_block(True)
        for s in range(n_ctx - 2):
            stack_ref[me ^ s] = piece_refs[s][...]
        part = stack_ref.shape[1] // 2
        for k, ref in enumerate(half_refs):
            at = pl.multiple_of((bit if k % 2 == 0 else 1 - bit) * part, part)
            stack_ref[me ^ (n_ctx - 2 + k // 2), pl.ds(at, part), :] = ref[...]
    for slot in range(order_ref.shape[0]):
        inverse_ref[order_ref[slot]] = slot
    block = order_ref[me * 2 + mine]
    reach_blocks = reach // half
    first = block - reach_blocks
    oldest = jnp.maximum(first, 0) * half + half - 1
    needed = (first >= 0) & (seg_ref[block * half] == seg_ref[oldest])
    order = [reach_blocks] + list(range(1, reach_blocks)) + [0]
    slots = [inverse_ref[jnp.maximum(first + w, 0)] for w in order]

    left = lax.broadcasted_iota(jnp.int32, (key_width, LANES), 1) < half

    def keys_into(target_ref, c, lanes):
        near, away = [slots[min(2 * c + side, reach_blocks)] for side in (0, 1)]
        first_tile = stack_ref[near >> 1, :key_width, :]
        second_tile = stack_ref[away >> 1, :key_width, :]
        turned = pltpu.roll(jnp.where(left, second_tile, first_tile), half, 1)
        both = jnp.where(
            left, jnp.where((near & 1) == 0, first_tile, turned), jnp.where((away & 1) == 1, second_tile, turned)
        )
        target_ref[0, :key_width, lanes] = both
        target_ref[1, key_pad - key_width :, lanes] = both

    def index_keys_into(target_ref, w, at):
        start = pl.multiple_of(key_width + (slots[w] & 1) * half, half)
        target_ref[at : at + half, :] = stack_ref[slots[w] >> 1, pl.ds(start, half), :]

    main_ref[0, key_width:, :] = jnp.zeros((key_pad - key_width, reach), main_ref.dtype)
    main_ref[1, : key_pad - key_width, :] = jnp.zeros((key_pad - key_width, reach), main_ref.dtype)
    for c in range(reach // LANES):
        keys_into(main_ref, c, slice(c * LANES, (c + 1) * LANES))

    row_id = lax.broadcasted_iota(jnp.int32, (half, LANES), 0)
    lane_id = lax.broadcasted_iota(jnp.int32, (half, LANES), 1)
    own_low = (lane_id <= row_id) | (lane_id >= half) | jnp.logical_not(needed)
    bias = bias_ref[mine]

    heads = query_ref.shape[1] // key_width
    stacked_queries = []
    for parity in (0, 1):
        starts = [g * 2 * key_width + parity * (2 * key_width - key_pad) for g in range(heads // 2)]
        stacked_queries.append(lambda starts=starts: jnp.concatenate([query_ref[rows_here, at : at + key_pad] for at in starts], axis=0))

    def index_lhs(ref):
        return jnp.concatenate([ref[:, j * idim : (j + 1) * idim] for j in range(ref.shape[1] // idim - 1)], axis=0)

    if keep:
        for w in range(reach_blocks):
            index_keys_into(index_main, w, w * half)

    @pl.when(needed)
    def _():
        tail_ref[0, key_width:, :] = jnp.zeros((key_pad - key_width, LANES), tail_ref.dtype)
        tail_ref[1, : key_pad - key_width, :] = jnp.zeros((key_pad - key_width, LANES), tail_ref.dtype)
        keys_into(tail_ref, reach // LANES, slice(0, LANES))
        for parity in (0, 1):
            raw_ref[parity] = lax.dot_general(
                stacked_queries[parity](), tail_ref[parity], (((1,), (0,)), ((), ())), preferred_element_type=jnp.float32
            )
        if keep:
            index_keys_into(index_tail, reach_blocks, 0)
            index_tail[half:, :] = jnp.zeros((LANES - half, idim), index_tail.dtype)
            for k, ref in enumerate(index_query_refs):
                index_raw[k] = lax.dot_general(
                    index_lhs(ref), index_tail[...], (((1,), (1,)), ((), ())), preferred_element_type=jnp.float32
                )

    groups = 2 * max(1, heads // 2 // 4)
    each = heads // groups

    def matmul(k):
        parity = k % 2
        starts = [(g + k // 2 * each) * 2 * key_width + parity * (2 * key_width - key_pad) for g in range(each)]
        lhs = jnp.concatenate([query_ref[rows_here, at : at + key_pad] for at in starts], axis=0)
        main_raw[k % 2] = lax.dot_general(
            lhs, main_ref[parity], (((1,), (0,)), ((), ())), preferred_element_type=jnp.float32
        )

    def softmax(k, total):
        for g in range(each):
            tail = raw_ref[k % 2, (g + k // 2 * each) * half : (g + k // 2 * each + 1) * half, :]
            scores = ring_fold(own_low, main_raw[k % 2, g * half : (g + 1) * half, :], tail) + bias
            row_max = jnp.max(scores, axis=1, keepdims=True)
            powers = jnp.exp2((scores - row_max) * (score_scale * math.log2(math.e)))
            share = 1.0 / jnp.sum(powers, axis=1, keepdims=True)
            total = total + powers * share
        return total

    total = jnp.zeros((half, reach), jnp.float32)
    matmul(0)
    for k in range(1, groups + 1):
        if k < groups:
            matmul(k)
        total = softmax(k - 1, total)
    out_refs[0][...] = total

    if keep:
        total = jnp.zeros((half, reach), jnp.float32)
        for k, ref in enumerate(index_query_refs):
            lhs = index_lhs(ref)
            dots = lax.dot_general(lhs, index_main[...], (((1,), (1,)), ((), ())), preferred_element_type=jnp.float32)
            gains = ref[:, lhs.shape[0] // half * idim :].astype(jnp.float32)
            for j in range(lhs.shape[0] // half):
                here = slice(j * half, (j + 1) * half)
                folded = ring_fold(own_low, dots[here, :], index_raw[k, here, :])
                total = total + gains[:, j : j + 1] * jnp.maximum(folded, 0.0)
        out_refs[1][...] = jnp.where(bias == 0.0, total, 0.0)


def loss_kernel(sizes, bias_ref, *refs):
    half, total_heads = sizes
    value_refs, out_ref = refs[:-1], refs[-1]
    mine = own_block(True)
    visible = bias_ref[mine] == 0.0
    target = functools.reduce(jnp.add, [ref[0] for ref in value_refs]) * (1.0 / total_heads)
    index_score = functools.reduce(jnp.add, [ref[1] for ref in value_refs])
    masked = jnp.where(visible, index_score, hidden)
    row_max = jnp.max(masked, axis=1, keepdims=True)
    exp_sum = jnp.sum(jnp.where(visible, jnp.exp(masked - row_max), 0.0), axis=1, keepdims=True)
    positive = target > 0.0
    logs = jnp.log(jnp.where(positive, target, 1.0))
    entropy_sum = jnp.sum(jnp.where(positive, target * logs, 0.0), axis=1, keepdims=True)
    cross_sum = jnp.sum(jnp.where(visible, target * index_score, 0.0), axis=1, keepdims=True)
    target_sum = jnp.sum(target, axis=1, keepdims=True)
    column = entropy_sum - cross_sum + (row_max + jnp.log(exp_sum)) * target_sum
    rows = out_ref.shape[1]
    row_id = lax.broadcasted_iota(jnp.int32, (half, rows), 0)
    lane_id = lax.broadcasted_iota(jnp.int32, (half, rows), 1)
    out_ref[...] = jnp.sum(jnp.where(row_id + mine * half == lane_id, column, 0.0), axis=0, keepdims=True)


def per_device(
    latent_keys, index_keys, main_query, index_query, index_weight, segment_ids, block_order
):
    n_ctx, n_head = lax.axis_size("ctx"), lax.axis_size("head")
    rows, key_width = latent_keys.shape
    idim = index_keys.shape[1]
    seq_len = segment_ids.shape[0]
    half = seq_len // block_order.shape[0]
    reach = seq_len // 4
    heads = main_query.shape[1] // key_width
    key_pad = -(-key_width // LANES) * LANES
    vmem = pl.BlockSpec(memory_space=pltpu.VMEM)
    smem = pl.BlockSpec(memory_space=pltpu.SMEM)
    hbm = pl.BlockSpec(memory_space=pltpu.HBM)
    index_heads = index_weight.shape[1]

    def far(x):
        return pltpu.with_memory_space_constraint(x, pltpu.HBM)

    packed, part = pl.pallas_call(
        pack_kernel,
        out_shape=(
            jax.ShapeDtypeStruct((key_width + idim, rows), latent_keys.dtype),
            jax.ShapeDtypeStruct(((key_width + idim) // 2, rows), latent_keys.dtype),
        ),
        in_specs=[hbm, hbm],
        out_specs=(vmem, vmem),
        scratch_shapes=[pltpu.SemaphoreType.DMA((4,))],
        compiler_params=pltpu.CompilerParams(vmem_limit_bytes=2 << 20),
        name="pack",
    )(far(latent_keys.T), far(index_keys))
    last = n_ctx // 2 - 1
    corner = swap(part, "ctx", 2 * last)
    own_core = []
    for s in reversed(range(1, last)):
        own_core.append(swap(packed, "ctx", 2 * s))
    corner_rest = swap(corner, "head", 1)
    pieces = []
    for piece in [packed] + own_core[::-1]:
        pieces += [piece, swap(piece, "ctx", 1)]
    pieces += [corner, corner_rest, swap(corner, "ctx", 1), swap(corner_rest, "ctx", 1)]
    seg_table = segment_ids.reshape(seq_len // LANES, LANES)

    copies = 8
    index_row = (half, index_query.shape[1] + LANES)
    bias, near_query, keep_query, give_query = pl.pallas_call(
        functools.partial(prelude_kernel, (half, reach, copies)),
        out_shape=(
            jax.ShapeDtypeStruct((2, half, reach), jnp.float32),
            jax.ShapeDtypeStruct(main_query.shape, main_query.dtype),
            jax.ShapeDtypeStruct(index_row, index_query.dtype),
            jax.ShapeDtypeStruct(index_row, index_query.dtype),
        ),
        in_specs=[hbm] * 5,
        out_specs=(vmem,) * 4,
        scratch_shapes=[
            pltpu.SMEM(block_order.shape, jnp.int32),
            pltpu.VMEM(seg_table.shape, jnp.int32),
            pltpu.VMEM((index_heads, rows), index_weight.dtype),
            pltpu.SemaphoreType.DMA((copies + 5,)),
        ],
        compiler_params=pltpu.CompilerParams(vmem_limit_bytes=12 << 20),
        cost_estimate=pl.CostEstimate(flops=1 << 20, bytes_accessed=10 << 20, transcendentals=0),
        name="prelude",
    )(far(block_order), far(seg_table), far(index_weight.T), far(main_query), far(index_query))
    taken_query = swap(give_query, "head", 1)

    stack = jax.ShapeDtypeStruct((n_ctx, key_width + idim, rows), packed.dtype)

    def block_sums(keep, keys):
        sums = jax.ShapeDtypeStruct((half, reach), jnp.float32)
        index_queries = [keep_query, taken_query] if keep else []
        return pl.pallas_call(
            functools.partial(block_kernel, (n_ctx, half, reach, key_width, idim), keep),
            out_shape=(sums, sums) if keep else (sums, stack),
            in_specs=[smem, smem] + [vmem] * (2 + len(index_queries) + len(keys)),
            out_specs=(vmem, vmem),
            scratch_shapes=[
                pltpu.VMEM((2, key_pad, reach), jnp.bfloat16),
                pltpu.VMEM((2, key_pad, LANES), jnp.bfloat16),
                pltpu.VMEM((reach, idim), jnp.bfloat16),
                pltpu.VMEM((LANES, idim), jnp.bfloat16),
                pltpu.VMEM((2, heads // 2 * half, LANES), jnp.float32),
                pltpu.VMEM((2, index_heads * half, LANES), jnp.float32),
                pltpu.VMEM((2, min(4, heads // 2) * half, reach), jnp.float32),
                pltpu.SMEM((block_order.shape[0],), jnp.int32),
            ],
            compiler_params=pltpu.CompilerParams(vmem_limit_bytes=28 << 20),
            cost_estimate=pl.CostEstimate(
                flops=2 * half * reach * heads * key_pad, bytes_accessed=4 << 20, transcendentals=0
            ),
            name="keep_sums" if keep else "give_sums",
        )(block_order, segment_ids, bias, near_query, *index_queries, *keys)

    given, key_stack = block_sums(False, pieces)
    kept, index_sums = block_sums(True, [key_stack])
    value = jnp.stack([kept + swap(given, "head", 1), index_sums])
    distances = [1 << k for k in range(1, n_head.bit_length() - 1)]
    for distance in distances[:-1]:
        value = value + swap(value, "head", distance)
    values = [value] + [swap(value, "head", distance) for distance in distances[-1:]]
    loss = pl.pallas_call(
        functools.partial(loss_kernel, (half, heads * n_head)),
        out_shape=jax.ShapeDtypeStruct((1, rows), jnp.float32),
        in_specs=[vmem] * (1 + len(values)),
        out_specs=vmem,
        compiler_params=pltpu.CompilerParams(vmem_limit_bytes=8 << 20),
        name="row_losses",
    )(bias, *values)
    return (loss + swap(loss, "head", 1)).reshape(rows)


def solution(mesh):
    in_specs = (
        P("ctx", None),
        P("ctx", None),
        P("ctx", "head"),
        P("ctx", "head"),
        P("ctx", "head"),
        P(),
        P(),
    )
    return jax.shard_map(per_device, mesh=mesh, in_specs=in_specs, out_specs=P("ctx"), check_vma=False)
```

```python
import functools
import math

import jax
import jax.numpy as jnp
from jax import lax
from jax.experimental import pallas as pl
from jax.experimental.pallas import tpu as pltpu
from jax.sharding import PartitionSpec as P


LANES = 128
score_scale = 192.0 ** (-0.5)
hidden = -1e30


def swap(x, axis, distance):
    size = lax.axis_size(axis)
    return lax.ppermute(x, axis, [(i, i ^ distance) for i in range(size)])


def window_masks(block, reach, half, seg_ref):
    table_rows = seg_ref.shape[0]
    first = block - reach // half
    row0 = lax.div(first + 2 * table_rows, 2) - table_rows
    pieces = []
    for k in range(reach // LANES + 2):
        row = jnp.clip(row0 + k, 0, table_rows - 1)
        pieces.append(seg_ref[pl.ds(row, 1), :].astype(jnp.float32))
    wide = jnp.concatenate(pieces, axis=1)
    width = wide.shape[1]
    moved = pltpu.roll(wide, width - half, 1)
    odd = lax.rem(first + 2 * table_rows, 2)
    wide = jnp.where(odd == 1, moved, wide)
    tail_seg = jnp.broadcast_to(wide[:, reach : reach + LANES], (half, LANES))
    head_seg = jnp.broadcast_to(wide[:, :LANES], (half, LANES))
    row_id = lax.broadcasted_iota(jnp.int32, (half, LANES), 0)
    lane_id = lax.broadcasted_iota(jnp.int32, (half, LANES), 1)
    query_seg = jnp.sum(jnp.where(row_id == lane_id, tail_seg, 0.0), axis=1, keepdims=True)
    in_tail = (lane_id <= row_id) & (lane_id < half)
    key_seg = jnp.concatenate(
        [jnp.where(in_tail, tail_seg, head_seg), jnp.broadcast_to(wide[:, LANES:reach], (half, reach - LANES))], axis=1
    )
    place = lax.broadcasted_iota(jnp.int32, (half, reach), 1)
    rows_full = lax.broadcasted_iota(jnp.int32, (half, reach), 0)
    tail_full = (place <= rows_full) & (place < half)
    position = first * half + place + jnp.where(tail_full, reach, 0)
    visible = (key_seg == query_seg) & (position >= 0)
    return in_tail, visible


def ring_fold(own_low, main, tail):
    low = jnp.where(own_low, main[:, :LANES], tail)
    return jnp.concatenate([low, main[:, LANES:]], axis=1)


def own_block(keep):
    bit = lax.axis_index("head") & 1
    return bit if keep else 1 - bit


def block_rows(keep, half):
    return pl.ds(pl.multiple_of(own_block(keep) * half, half), half)


def pack_kernel(latent_hbm, index_hbm, out_ref, part_ref, sems):
    width = latent_hbm.shape[0]
    part = part_ref.shape[0]
    bit = own_block(True)
    quarter = width // 4
    whole = [pltpu.make_async_copy(index_hbm, out_ref.at[width:, :], sems.at[0])]
    for c in range(4):
        here = slice(c * quarter, (c + 1) * quarter)
        whole.append(pltpu.make_async_copy(latent_hbm.at[here, :], out_ref.at[here, :], sems.at[4 + c]))
    low = [pltpu.make_async_copy(latent_hbm.at[:part, :], part_ref, sems.at[2])]
    high = [
        pltpu.make_async_copy(latent_hbm.at[part:, :], part_ref.at[: width - part, :], sems.at[2]),
        pltpu.make_async_copy(index_hbm, part_ref.at[width - part :, :], sems.at[3]),
    ]

    def each(copies, act):
        for copy in copies:
            act(copy)

    for act in (lambda copy: copy.start(), lambda copy: copy.wait()):
        each(whole, act)
        pl.when(bit == 0)(functools.partial(each, low, act))
        pl.when(bit == 1)(functools.partial(each, high, act))


def prelude_kernel(sizes, order_hbm, seg_hbm, weight_hbm, query_hbm, index_query_hbm,
                   bias_ref, query_ref, keep_ref, give_ref, order_ref, seg_ref, weight_ref, sems):
    half, reach, copies = sizes
    rows = query_ref.shape[0]
    width = index_query_hbm.shape[1]
    small = [
        pltpu.make_async_copy(order_hbm, order_ref, sems.at[0]),
        pltpu.make_async_copy(seg_hbm, seg_ref, sems.at[1]),
        pltpu.make_async_copy(weight_hbm, weight_ref, sems.at[2]),
    ]
    large = [
        pltpu.make_async_copy(index_query_hbm.at[block_rows(False, half), :], give_ref.at[:, :width], sems.at[3]),
        pltpu.make_async_copy(index_query_hbm.at[block_rows(True, half), :], keep_ref.at[:, :width], sems.at[4]),
    ]
    for c in range(copies):
        part = slice(c * (rows // copies), (c + 1) * (rows // copies))
        large.append(pltpu.make_async_copy(query_hbm.at[part, :], query_ref.at[part, :], sems.at[5 + c]))
    for copy in small + large:
        copy.start()
    for copy in small:
        copy.wait()
    me = lax.axis_index("ctx")
    for i in range(2):
        _, visible = window_masks(order_ref[me * 2 + i], reach, half, seg_ref)
        bias_ref[i] = jnp.where(visible, 0.0, hidden)
    gains = jnp.transpose(weight_ref[...].astype(jnp.float32), (1, 0))
    gains = jnp.concatenate([gains, jnp.zeros((rows, LANES - gains.shape[1]), gains.dtype)], axis=1)
    gains = gains.astype(keep_ref.dtype)
    first_kept = own_block(True) == 0
    keep_ref[:, width:] = jnp.where(first_kept, gains[:half], gains[half:])
    give_ref[:, width:] = jnp.where(first_kept, gains[half:], gains[:half])
    for copy in large:
        copy.wait()


def block_kernel(sizes, keep, order_ref, seg_ref, bias_ref, query_ref, *refs):
    n_ctx, half, reach, key_width, idim = sizes
    n_index = 2 if keep else 0
    index_query_refs, refs = refs[:n_index], refs[n_index:]
    if keep:
        stack_ref, refs = refs[0], refs[1:]
    else:
        piece_refs, half_refs, refs = refs[: n_ctx - 2], refs[n_ctx - 2 : n_ctx + 2], refs[n_ctx + 2 :]
    out_refs, refs = refs[:2], refs[2:]
    main_ref, tail_ref, index_main, index_tail, raw_ref, index_raw, main_raw, inverse_ref = refs
    key_pad = main_ref.shape[1]
    me = lax.axis_index("ctx")
    mine = own_block(keep)
    rows_here = block_rows(keep, half)
    if not keep:
        stack_ref = out_refs[1]
        bit = own_block(True)
        for s in range(n_ctx - 2):
            stack_ref[me ^ s] = piece_refs[s][...]
        part = stack_ref.shape[1] // 2
        for k, ref in enumerate(half_refs):
            at = pl.multiple_of((bit if k % 2 == 0 else 1 - bit) * part, part)
            stack_ref[me ^ (n_ctx - 2 + k // 2), pl.ds(at, part), :] = ref[...]
    for slot in range(order_ref.shape[0]):
        inverse_ref[order_ref[slot]] = slot
    block = order_ref[me * 2 + mine]
    reach_blocks = reach // half
    first = block - reach_blocks
    oldest = jnp.maximum(first, 0) * half + half - 1
    needed = (first >= 0) & (seg_ref[block * half] == seg_ref[oldest])
    order = [reach_blocks] + list(range(1, reach_blocks)) + [0]
    slots = [inverse_ref[jnp.maximum(first + w, 0)] for w in order]

    left = lax.broadcasted_iota(jnp.int32, (key_width, LANES), 1) < half

    def keys_into(target_ref, c, lanes):
        near, away = [slots[min(2 * c + side, reach_blocks)] for side in (0, 1)]
        first_tile = stack_ref[near >> 1, :key_width, :]
        second_tile = stack_ref[away >> 1, :key_width, :]
        turned = pltpu.roll(jnp.where(left, second_tile, first_tile), half, 1)
        both = jnp.where(
            left, jnp.where((near & 1) == 0, first_tile, turned), jnp.where((away & 1) == 1, second_tile, turned)
        )
        target_ref[0, :key_width, lanes] = both
        target_ref[1, key_pad - key_width :, lanes] = both

    def index_keys_into(target_ref, w, at):
        start = pl.multiple_of(key_width + (slots[w] & 1) * half, half)
        target_ref[at : at + half, :] = stack_ref[slots[w] >> 1, pl.ds(start, half), :]

    main_ref[0, key_width:, :] = jnp.zeros((key_pad - key_width, reach), main_ref.dtype)
    main_ref[1, : key_pad - key_width, :] = jnp.zeros((key_pad - key_width, reach), main_ref.dtype)
    for c in range(reach // LANES):
        keys_into(main_ref, c, slice(c * LANES, (c + 1) * LANES))

    row_id = lax.broadcasted_iota(jnp.int32, (half, LANES), 0)
    lane_id = lax.broadcasted_iota(jnp.int32, (half, LANES), 1)
    own_low = (lane_id <= row_id) | (lane_id >= half) | jnp.logical_not(needed)
    bias = bias_ref[mine]

    heads = query_ref.shape[1] // key_width
    stacked_queries = []
    for parity in (0, 1):
        starts = [g * 2 * key_width + parity * (2 * key_width - key_pad) for g in range(heads // 2)]
        stacked_queries.append(lambda starts=starts: jnp.concatenate([query_ref[rows_here, at : at + key_pad] for at in starts], axis=0))

    def index_lhs(ref):
        return jnp.concatenate([ref[:, j * idim : (j + 1) * idim] for j in range(ref.shape[1] // idim - 1)], axis=0)

    if keep:
        for w in range(reach_blocks):
            index_keys_into(index_main, w, w * half)

    @pl.when(needed)
    def _():
        tail_ref[0, key_width:, :] = jnp.zeros((key_pad - key_width, LANES), tail_ref.dtype)
        tail_ref[1, : key_pad - key_width, :] = jnp.zeros((key_pad - key_width, LANES), tail_ref.dtype)
        keys_into(tail_ref, reach // LANES, slice(0, LANES))
        for parity in (0, 1):
            raw_ref[parity] = lax.dot_general(
                stacked_queries[parity](), tail_ref[parity], (((1,), (0,)), ((), ())), preferred_element_type=jnp.float32
            )
        if keep:
            index_keys_into(index_tail, reach_blocks, 0)
            index_tail[half:, :] = jnp.zeros((LANES - half, idim), index_tail.dtype)
            for k, ref in enumerate(index_query_refs):
                index_raw[k] = lax.dot_general(
                    index_lhs(ref), index_tail[...], (((1,), (1,)), ((), ())), preferred_element_type=jnp.float32
                )

    groups = 2 * max(1, heads // 2 // 4)
    each = heads // groups

    def matmul(k):
        parity = k % 2
        starts = [(g + k // 2 * each) * 2 * key_width + parity * (2 * key_width - key_pad) for g in range(each)]
        lhs = jnp.concatenate([query_ref[rows_here, at : at + key_pad] for at in starts], axis=0)
        main_raw[k % 2] = lax.dot_general(
            lhs, main_ref[parity], (((1,), (0,)), ((), ())), preferred_element_type=jnp.float32
        )

    def softmax(k, total):
        for g in range(each):
            tail = raw_ref[k % 2, (g + k // 2 * each) * half : (g + k // 2 * each + 1) * half, :]
            scores = ring_fold(own_low, main_raw[k % 2, g * half : (g + 1) * half, :], tail) + bias
            row_max = jnp.max(scores, axis=1, keepdims=True)
            powers = jnp.exp2((scores - row_max) * (score_scale * math.log2(math.e)))
            share = 1.0 / jnp.sum(powers, axis=1, keepdims=True)
            total = total + powers * share
        return total

    total = jnp.zeros((half, reach), jnp.float32)
    matmul(0)
    for k in range(1, groups + 1):
        if k < groups:
            matmul(k)
        total = softmax(k - 1, total)
    out_refs[0][...] = total

    if keep:
        total = jnp.zeros((half, reach), jnp.float32)
        for k, ref in enumerate(index_query_refs):
            lhs = index_lhs(ref)
            dots = lax.dot_general(lhs, index_main[...], (((1,), (1,)), ((), ())), preferred_element_type=jnp.float32)
            gains = ref[:, lhs.shape[0] // half * idim :].astype(jnp.float32)
            for j in range(lhs.shape[0] // half):
                here = slice(j * half, (j + 1) * half)
                folded = ring_fold(own_low, dots[here, :], index_raw[k, here, :])
                total = total + gains[:, j : j + 1] * jnp.maximum(folded, 0.0)
        out_refs[1][...] = jnp.where(bias == 0.0, total, 0.0)


def loss_kernel(sizes, bias_ref, *refs):
    half, total_heads = sizes
    value_refs, out_ref = refs[:-1], refs[-1]
    mine = own_block(True)
    visible = bias_ref[mine] == 0.0
    target = functools.reduce(jnp.add, [ref[0] for ref in value_refs]) * (1.0 / total_heads)
    index_score = functools.reduce(jnp.add, [ref[1] for ref in value_refs])
    masked = jnp.where(visible, index_score, hidden)
    row_max = jnp.max(masked, axis=1, keepdims=True)
    exp_sum = jnp.sum(jnp.where(visible, jnp.exp(masked - row_max), 0.0), axis=1, keepdims=True)
    positive = target > 0.0
    logs = jnp.log(jnp.where(positive, target, 1.0))
    entropy_sum = jnp.sum(jnp.where(positive, target * logs, 0.0), axis=1, keepdims=True)
    cross_sum = jnp.sum(jnp.where(visible, target * index_score, 0.0), axis=1, keepdims=True)
    target_sum = jnp.sum(target, axis=1, keepdims=True)
    column = entropy_sum - cross_sum + (row_max + jnp.log(exp_sum)) * target_sum
    rows = out_ref.shape[1]
    row_id = lax.broadcasted_iota(jnp.int32, (half, rows), 0)
    lane_id = lax.broadcasted_iota(jnp.int32, (half, rows), 1)
    out_ref[...] = jnp.sum(jnp.where(row_id + mine * half == lane_id, column, 0.0), axis=0, keepdims=True)


def per_device(
    latent_keys, index_keys, main_query, index_query, index_weight, segment_ids, block_order
):
    n_ctx, n_head = lax.axis_size("ctx"), lax.axis_size("head")
    rows, key_width = latent_keys.shape
    idim = index_keys.shape[1]
    seq_len = segment_ids.shape[0]
    half = seq_len // block_order.shape[0]
    reach = seq_len // 4
    heads = main_query.shape[1] // key_width
    key_pad = -(-key_width // LANES) * LANES
    vmem = pl.BlockSpec(memory_space=pltpu.VMEM)
    smem = pl.BlockSpec(memory_space=pltpu.SMEM)
    hbm = pl.BlockSpec(memory_space=pltpu.HBM)
    index_heads = index_weight.shape[1]

    def far(x):
        return pltpu.with_memory_space_constraint(x, pltpu.HBM)

    packed, part = pl.pallas_call(
        pack_kernel,
        out_shape=(
            jax.ShapeDtypeStruct((key_width + idim, rows), latent_keys.dtype),
            jax.ShapeDtypeStruct(((key_width + idim) // 2, rows), latent_keys.dtype),
        ),
        in_specs=[hbm, hbm],
        out_specs=(vmem, vmem),
        scratch_shapes=[pltpu.SemaphoreType.DMA((8,))],
        compiler_params=pltpu.CompilerParams(vmem_limit_bytes=2 << 20),
        name="pack",
    )(far(latent_keys.T), far(index_keys))
    last = n_ctx // 2 - 1
    corner = swap(part, "ctx", 2 * last)
    own_core = []
    for s in reversed(range(1, last)):
        own_core.append(swap(packed, "ctx", 2 * s))
    corner_rest = swap(corner, "head", 1)
    pieces = []
    for piece in [packed] + own_core[::-1]:
        pieces += [piece, swap(piece, "ctx", 1)]
    pieces += [corner, corner_rest, swap(corner, "ctx", 1), swap(corner_rest, "ctx", 1)]
    seg_table = segment_ids.reshape(seq_len // LANES, LANES)

    copies = 8
    index_row = (half, index_query.shape[1] + LANES)
    bias, near_query, keep_query, give_query = pl.pallas_call(
        functools.partial(prelude_kernel, (half, reach, copies)),
        out_shape=(
            jax.ShapeDtypeStruct((2, half, reach), jnp.float32),
            jax.ShapeDtypeStruct(main_query.shape, main_query.dtype),
            jax.ShapeDtypeStruct(index_row, index_query.dtype),
            jax.ShapeDtypeStruct(index_row, index_query.dtype),
        ),
        in_specs=[hbm] * 5,
        out_specs=(vmem,) * 4,
        scratch_shapes=[
            pltpu.SMEM(block_order.shape, jnp.int32),
            pltpu.VMEM(seg_table.shape, jnp.int32),
            pltpu.VMEM((index_heads, rows), index_weight.dtype),
            pltpu.SemaphoreType.DMA((copies + 5,)),
        ],
        compiler_params=pltpu.CompilerParams(vmem_limit_bytes=12 << 20),
        cost_estimate=pl.CostEstimate(flops=1 << 20, bytes_accessed=10 << 20, transcendentals=0),
        name="prelude",
    )(far(block_order), far(seg_table), far(index_weight.T), far(main_query), far(index_query))
    taken_query = swap(give_query, "head", 1)

    stack = jax.ShapeDtypeStruct((n_ctx, key_width + idim, rows), packed.dtype)

    def block_sums(keep, keys):
        sums = jax.ShapeDtypeStruct((half, reach), jnp.float32)
        index_queries = [keep_query, taken_query] if keep else []
        return pl.pallas_call(
            functools.partial(block_kernel, (n_ctx, half, reach, key_width, idim), keep),
            out_shape=(sums, sums) if keep else (sums, stack),
            in_specs=[smem, smem] + [vmem] * (2 + len(index_queries) + len(keys)),
            out_specs=(vmem, vmem),
            scratch_shapes=[
                pltpu.VMEM((2, key_pad, reach), jnp.bfloat16),
                pltpu.VMEM((2, key_pad, LANES), jnp.bfloat16),
                pltpu.VMEM((reach, idim), jnp.bfloat16),
                pltpu.VMEM((LANES, idim), jnp.bfloat16),
                pltpu.VMEM((2, heads // 2 * half, LANES), jnp.float32),
                pltpu.VMEM((2, index_heads * half, LANES), jnp.float32),
                pltpu.VMEM((2, min(4, heads // 2) * half, reach), jnp.float32),
                pltpu.SMEM((block_order.shape[0],), jnp.int32),
            ],
            compiler_params=pltpu.CompilerParams(vmem_limit_bytes=28 << 20),
            cost_estimate=pl.CostEstimate(
                flops=2 * half * reach * heads * key_pad, bytes_accessed=4 << 20, transcendentals=0
            ),
            name="keep_sums" if keep else "give_sums",
        )(block_order, segment_ids, bias, near_query, *index_queries, *keys)

    given, key_stack = block_sums(False, pieces)
    kept, index_sums = block_sums(True, [key_stack])
    value = jnp.stack([kept + swap(given, "head", 1), index_sums])
    distances = [1 << k for k in range(1, n_head.bit_length() - 1)]
    for distance in distances[:-1]:
        value = value + swap(value, "head", distance)
    values = [value] + [swap(value, "head", distance) for distance in distances[-1:]]
    loss = pl.pallas_call(
        functools.partial(loss_kernel, (half, heads * n_head)),
        out_shape=jax.ShapeDtypeStruct((1, rows), jnp.float32),
        in_specs=[vmem] * (1 + len(values)),
        out_specs=vmem,
        compiler_params=pltpu.CompilerParams(vmem_limit_bytes=8 << 20),
        name="row_losses",
    )(bias, *values)
    return (loss + swap(loss, "head", 1)).reshape(rows)


def solution(mesh):
    in_specs = (
        P("ctx", None),
        P("ctx", None),
        P("ctx", "head"),
        P("ctx", "head"),
        P("ctx", "head"),
        P(),
        P(),
    )
    return jax.shard_map(per_device, mesh=mesh, in_specs=in_specs, out_specs=P("ctx"), check_vma=False)
```

```python
import functools
import math

import jax
import jax.numpy as jnp
from jax import lax
from jax.experimental import pallas as pl
from jax.experimental.pallas import tpu as pltpu
from jax.sharding import PartitionSpec as P


LANES = 128
score_scale = 192.0 ** (-0.5)
hidden = -1e30


def swap(x, axis, distance):
    size = lax.axis_size(axis)
    return lax.ppermute(x, axis, [(i, i ^ distance) for i in range(size)])


def window_masks(block, reach, half, seg_ref):
    table_rows = seg_ref.shape[0]
    first = block - reach // half
    row0 = lax.div(first + 2 * table_rows, 2) - table_rows
    pieces = []
    for k in range(reach // LANES + 2):
        row = jnp.clip(row0 + k, 0, table_rows - 1)
        pieces.append(seg_ref[pl.ds(row, 1), :].astype(jnp.float32))
    wide = jnp.concatenate(pieces, axis=1)
    width = wide.shape[1]
    moved = pltpu.roll(wide, width - half, 1)
    odd = lax.rem(first + 2 * table_rows, 2)
    wide = jnp.where(odd == 1, moved, wide)
    tail_seg = jnp.broadcast_to(wide[:, reach : reach + LANES], (half, LANES))
    head_seg = jnp.broadcast_to(wide[:, :LANES], (half, LANES))
    row_id = lax.broadcasted_iota(jnp.int32, (half, LANES), 0)
    lane_id = lax.broadcasted_iota(jnp.int32, (half, LANES), 1)
    query_seg = jnp.sum(jnp.where(row_id == lane_id, tail_seg, 0.0), axis=1, keepdims=True)
    in_tail = (lane_id <= row_id) & (lane_id < half)
    key_seg = jnp.concatenate(
        [jnp.where(in_tail, tail_seg, head_seg), jnp.broadcast_to(wide[:, LANES:reach], (half, reach - LANES))], axis=1
    )
    place = lax.broadcasted_iota(jnp.int32, (half, reach), 1)
    rows_full = lax.broadcasted_iota(jnp.int32, (half, reach), 0)
    tail_full = (place <= rows_full) & (place < half)
    position = first * half + place + jnp.where(tail_full, reach, 0)
    visible = (key_seg == query_seg) & (position >= 0)
    return in_tail, visible


def ring_fold(own_low, main, tail):
    low = jnp.where(own_low, main[:, :LANES], tail)
    return jnp.concatenate([low, main[:, LANES:]], axis=1)


def own_block(keep):
    bit = lax.axis_index("head") & 1
    return bit if keep else 1 - bit


def block_rows(keep, half):
    return pl.ds(pl.multiple_of(own_block(keep) * half, half), half)


def pack_kernel(latent_hbm, index_hbm, out_ref, part_ref, sems):
    width = latent_hbm.shape[0]
    part = part_ref.shape[0]
    bit = own_block(True)
    quarter = width // 4
    whole = [pltpu.make_async_copy(index_hbm, out_ref.at[width:, :], sems.at[0])]
    for c in range(4):
        here = slice(c * quarter, (c + 1) * quarter)
        whole.append(pltpu.make_async_copy(latent_hbm.at[here, :], out_ref.at[here, :], sems.at[4 + c]))
    low = [pltpu.make_async_copy(latent_hbm.at[:part, :], part_ref, sems.at[2])]
    high = [
        pltpu.make_async_copy(latent_hbm.at[part:, :], part_ref.at[: width - part, :], sems.at[2]),
        pltpu.make_async_copy(index_hbm, part_ref.at[width - part :, :], sems.at[3]),
    ]

    def each(copies, act):
        for copy in copies:
            act(copy)

    for act in (lambda copy: copy.start(), lambda copy: copy.wait()):
        each(whole, act)
        pl.when(bit == 0)(functools.partial(each, low, act))
        pl.when(bit == 1)(functools.partial(each, high, act))


def prelude_kernel(sizes, order_hbm, seg_hbm, weight_hbm, query_hbm, index_query_hbm,
                   bias_ref, query_ref, keep_ref, give_ref, order_ref, seg_ref, weight_ref, sems):
    half, reach, copies = sizes
    rows = query_ref.shape[0]
    width = index_query_hbm.shape[1]
    small = [
        pltpu.make_async_copy(order_hbm, order_ref, sems.at[0]),
        pltpu.make_async_copy(seg_hbm, seg_ref, sems.at[1]),
        pltpu.make_async_copy(weight_hbm, weight_ref, sems.at[2]),
    ]
    large = [
        pltpu.make_async_copy(index_query_hbm.at[block_rows(False, half), :], give_ref.at[:, :width], sems.at[3]),
        pltpu.make_async_copy(index_query_hbm.at[block_rows(True, half), :], keep_ref.at[:, :width], sems.at[4]),
    ]
    for c in range(copies):
        part = slice(c * (rows // copies), (c + 1) * (rows // copies))
        large.append(pltpu.make_async_copy(query_hbm.at[part, :], query_ref.at[part, :], sems.at[5 + c]))
    for copy in small + large:
        copy.start()
    for copy in small:
        copy.wait()
    me = lax.axis_index("ctx")
    for i in range(2):
        _, visible = window_masks(order_ref[me * 2 + i], reach, half, seg_ref)
        bias_ref[i] = jnp.where(visible, 0.0, hidden)
    gains = jnp.transpose(weight_ref[...].astype(jnp.float32), (1, 0))
    gains = jnp.concatenate([gains, jnp.zeros((rows, LANES - gains.shape[1]), gains.dtype)], axis=1)
    gains = gains.astype(keep_ref.dtype)
    first_kept = own_block(True) == 0
    keep_ref[:, width:] = jnp.where(first_kept, gains[:half], gains[half:])
    give_ref[:, width:] = jnp.where(first_kept, gains[half:], gains[:half])
    for copy in large:
        copy.wait()


def block_kernel(sizes, keep, order_ref, seg_ref, bias_ref, query_ref, *refs):
    n_ctx, half, reach, key_width, idim = sizes
    index_query_refs, refs = refs[:1], refs[1:]
    if keep:
        stack_ref, refs = refs[0], refs[1:]
    else:
        piece_refs, half_refs, refs = refs[: n_ctx - 2], refs[n_ctx - 2 : n_ctx + 2], refs[n_ctx + 2 :]
    out_ref, refs = refs[0], refs[1:]
    if not keep:
        stack_ref, refs = refs[0], refs[1:]
    main_ref, tail_ref, index_main, index_tail, raw_ref, index_raw, main_raw, inverse_ref = refs
    key_pad = main_ref.shape[1]
    me = lax.axis_index("ctx")
    mine = own_block(keep)
    rows_here = block_rows(keep, half)
    if not keep:
        bit = own_block(True)
        for s in range(n_ctx - 2):
            stack_ref[me ^ s] = piece_refs[s][...]
        part = stack_ref.shape[1] // 2
        for k, ref in enumerate(half_refs):
            at = pl.multiple_of((bit if k % 2 == 0 else 1 - bit) * part, part)
            stack_ref[me ^ (n_ctx - 2 + k // 2), pl.ds(at, part), :] = ref[...]
    for slot in range(order_ref.shape[0]):
        inverse_ref[order_ref[slot]] = slot
    block = order_ref[me * 2 + mine]
    reach_blocks = reach // half
    first = block - reach_blocks
    oldest = jnp.maximum(first, 0) * half + half - 1
    needed = (first >= 0) & (seg_ref[block * half] == seg_ref[oldest])
    order = [reach_blocks] + list(range(1, reach_blocks)) + [0]
    slots = [inverse_ref[jnp.maximum(first + w, 0)] for w in order]

    left = lax.broadcasted_iota(jnp.int32, (key_width, LANES), 1) < half

    def keys_into(target_ref, c, lanes):
        near, away = [slots[min(2 * c + side, reach_blocks)] for side in (0, 1)]
        first_tile = stack_ref[near >> 1, :key_width, :]
        second_tile = stack_ref[away >> 1, :key_width, :]
        turned = pltpu.roll(jnp.where(left, second_tile, first_tile), half, 1)
        both = jnp.where(
            left, jnp.where((near & 1) == 0, first_tile, turned), jnp.where((away & 1) == 1, second_tile, turned)
        )
        target_ref[0, :key_width, lanes] = both
        target_ref[1, key_pad - key_width :, lanes] = both

    def index_keys_into(target_ref, w, at):
        start = pl.multiple_of(key_width + (slots[w] & 1) * half, half)
        target_ref[at : at + half, :] = stack_ref[slots[w] >> 1, pl.ds(start, half), :]

    main_ref[0, key_width:, :] = jnp.zeros((key_pad - key_width, reach), main_ref.dtype)
    main_ref[1, : key_pad - key_width, :] = jnp.zeros((key_pad - key_width, reach), main_ref.dtype)
    for c in range(reach // LANES):
        keys_into(main_ref, c, slice(c * LANES, (c + 1) * LANES))

    row_id = lax.broadcasted_iota(jnp.int32, (half, LANES), 0)
    lane_id = lax.broadcasted_iota(jnp.int32, (half, LANES), 1)
    own_low = (lane_id <= row_id) | (lane_id >= half) | jnp.logical_not(needed)
    bias = bias_ref[mine]

    heads = query_ref.shape[1] // key_width
    stacked_queries = []
    for parity in (0, 1):
        starts = [g * 2 * key_width + parity * (2 * key_width - key_pad) for g in range(heads // 2)]
        stacked_queries.append(lambda starts=starts: jnp.concatenate([query_ref[rows_here, at : at + key_pad] for at in starts], axis=0))

    def index_lhs(ref):
        return jnp.concatenate([ref[:, j * idim : (j + 1) * idim] for j in range(ref.shape[1] // idim - 1)], axis=0)

    for w in range(reach_blocks):
        index_keys_into(index_main, w, w * half)

    @pl.when(needed)
    def _():
        tail_ref[0, key_width:, :] = jnp.zeros((key_pad - key_width, LANES), tail_ref.dtype)
        tail_ref[1, : key_pad - key_width, :] = jnp.zeros((key_pad - key_width, LANES), tail_ref.dtype)
        keys_into(tail_ref, reach // LANES, slice(0, LANES))
        for parity in (0, 1):
            raw_ref[parity] = lax.dot_general(
                stacked_queries[parity](), tail_ref[parity], (((1,), (0,)), ((), ())), preferred_element_type=jnp.float32
            )
        index_keys_into(index_tail, reach_blocks, 0)
        index_tail[half:, :] = jnp.zeros((LANES - half, idim), index_tail.dtype)
        for k, ref in enumerate(index_query_refs):
            index_raw[k] = lax.dot_general(
                index_lhs(ref), index_tail[...], (((1,), (1,)), ((), ())), preferred_element_type=jnp.float32
            )

    groups = 2 * max(1, heads // 2 // 4)
    each = heads // groups

    def matmul(k):
        parity = k % 2
        starts = [(g + k // 2 * each) * 2 * key_width + parity * (2 * key_width - key_pad) for g in range(each)]
        lhs = jnp.concatenate([query_ref[rows_here, at : at + key_pad] for at in starts], axis=0)
        main_raw[k % 2] = lax.dot_general(
            lhs, main_ref[parity], (((1,), (0,)), ((), ())), preferred_element_type=jnp.float32
        )

    def softmax(k, total):
        for g in range(each):
            tail = raw_ref[k % 2, (g + k // 2 * each) * half : (g + k // 2 * each + 1) * half, :]
            scores = ring_fold(own_low, main_raw[k % 2, g * half : (g + 1) * half, :], tail) + bias
            row_max = jnp.max(scores, axis=1, keepdims=True)
            powers = jnp.exp2((scores - row_max) * (score_scale * math.log2(math.e)))
            share = 1.0 / jnp.sum(powers, axis=1, keepdims=True)
            total = total + powers * share
        return total

    total = jnp.zeros((half, reach), jnp.float32)
    matmul(0)
    for k in range(1, groups + 1):
        if k < groups:
            matmul(k)
        total = softmax(k - 1, total)
    out_ref[0] = total

    total = jnp.zeros((half, reach), jnp.float32)
    for k, ref in enumerate(index_query_refs):
        lhs = index_lhs(ref)
        dots = lax.dot_general(lhs, index_main[...], (((1,), (1,)), ((), ())), preferred_element_type=jnp.float32)
        gains = ref[:, lhs.shape[0] // half * idim :].astype(jnp.float32)
        for j in range(lhs.shape[0] // half):
            here = slice(j * half, (j + 1) * half)
            folded = ring_fold(own_low, dots[here, :], index_raw[k, here, :])
            total = total + gains[:, j : j + 1] * jnp.maximum(folded, 0.0)
    out_ref[1] = jnp.where(bias == 0.0, total, 0.0)


def loss_kernel(sizes, bias_ref, *refs):
    half, total_heads = sizes
    value_refs, out_ref = refs[:-1], refs[-1]
    mine = own_block(True)
    visible = bias_ref[mine] == 0.0
    target = functools.reduce(jnp.add, [ref[0] for ref in value_refs]) * (1.0 / total_heads)
    index_score = functools.reduce(jnp.add, [ref[1] for ref in value_refs])
    masked = jnp.where(visible, index_score, hidden)
    row_max = jnp.max(masked, axis=1, keepdims=True)
    exp_sum = jnp.sum(jnp.where(visible, jnp.exp(masked - row_max), 0.0), axis=1, keepdims=True)
    positive = target > 0.0
    logs = jnp.log(jnp.where(positive, target, 1.0))
    entropy_sum = jnp.sum(jnp.where(positive, target * logs, 0.0), axis=1, keepdims=True)
    cross_sum = jnp.sum(jnp.where(visible, target * index_score, 0.0), axis=1, keepdims=True)
    target_sum = jnp.sum(target, axis=1, keepdims=True)
    column = entropy_sum - cross_sum + (row_max + jnp.log(exp_sum)) * target_sum
    rows = out_ref.shape[1]
    row_id = lax.broadcasted_iota(jnp.int32, (half, rows), 0)
    lane_id = lax.broadcasted_iota(jnp.int32, (half, rows), 1)
    out_ref[...] = jnp.sum(jnp.where(row_id + mine * half == lane_id, column, 0.0), axis=0, keepdims=True)


def per_device(
    latent_keys, index_keys, main_query, index_query, index_weight, segment_ids, block_order
):
    n_ctx, n_head = lax.axis_size("ctx"), lax.axis_size("head")
    rows, key_width = latent_keys.shape
    idim = index_keys.shape[1]
    seq_len = segment_ids.shape[0]
    half = seq_len // block_order.shape[0]
    reach = seq_len // 4
    heads = main_query.shape[1] // key_width
    key_pad = -(-key_width // LANES) * LANES
    vmem = pl.BlockSpec(memory_space=pltpu.VMEM)
    smem = pl.BlockSpec(memory_space=pltpu.SMEM)
    hbm = pl.BlockSpec(memory_space=pltpu.HBM)
    index_heads = index_weight.shape[1]

    def far(x):
        return pltpu.with_memory_space_constraint(x, pltpu.HBM)

    packed, part = pl.pallas_call(
        pack_kernel,
        out_shape=(
            jax.ShapeDtypeStruct((key_width + idim, rows), latent_keys.dtype),
            jax.ShapeDtypeStruct(((key_width + idim) // 2, rows), latent_keys.dtype),
        ),
        in_specs=[hbm, hbm],
        out_specs=(vmem, vmem),
        scratch_shapes=[pltpu.SemaphoreType.DMA((8,))],
        compiler_params=pltpu.CompilerParams(vmem_limit_bytes=2 << 20),
        name="pack",
    )(far(latent_keys.T), far(index_keys))
    last = n_ctx // 2 - 1
    corner = swap(part, "ctx", 2 * last)
    own_core = []
    for s in reversed(range(1, last)):
        own_core.append(swap(packed, "ctx", 2 * s))
    corner_rest = swap(corner, "head", 1)
    pieces = []
    for piece in [packed] + own_core[::-1]:
        pieces += [piece, swap(piece, "ctx", 1)]
    pieces += [corner, corner_rest, swap(corner, "ctx", 1), swap(corner_rest, "ctx", 1)]
    seg_table = segment_ids.reshape(seq_len // LANES, LANES)

    copies = 8
    index_row = (half, index_query.shape[1] + LANES)
    bias, near_query, keep_query, give_query = pl.pallas_call(
        functools.partial(prelude_kernel, (half, reach, copies)),
        out_shape=(
            jax.ShapeDtypeStruct((2, half, reach), jnp.float32),
            jax.ShapeDtypeStruct(main_query.shape, main_query.dtype),
            jax.ShapeDtypeStruct(index_row, index_query.dtype),
            jax.ShapeDtypeStruct(index_row, index_query.dtype),
        ),
        in_specs=[hbm] * 5,
        out_specs=(vmem,) * 4,
        scratch_shapes=[
            pltpu.SMEM(block_order.shape, jnp.int32),
            pltpu.VMEM(seg_table.shape, jnp.int32),
            pltpu.VMEM((index_heads, rows), index_weight.dtype),
            pltpu.SemaphoreType.DMA((copies + 5,)),
        ],
        compiler_params=pltpu.CompilerParams(vmem_limit_bytes=12 << 20),
        cost_estimate=pl.CostEstimate(flops=1 << 20, bytes_accessed=10 << 20, transcendentals=0),
        name="prelude",
    )(far(block_order), far(seg_table), far(index_weight.T), far(main_query), far(index_query))

    stack = jax.ShapeDtypeStruct((n_ctx, key_width + idim, rows), packed.dtype)

    def block_sums(keep, keys):
        sums = jax.ShapeDtypeStruct((2, half, reach), jnp.float32)
        index_query_here = keep_query if keep else give_query
        return pl.pallas_call(
            functools.partial(block_kernel, (n_ctx, half, reach, key_width, idim), keep),
            out_shape=sums if keep else (sums, stack),
            in_specs=[smem, smem] + [vmem] * (3 + len(keys)),
            out_specs=vmem if keep else (vmem, vmem),
            scratch_shapes=[
                pltpu.VMEM((2, key_pad, reach), jnp.bfloat16),
                pltpu.VMEM((2, key_pad, LANES), jnp.bfloat16),
                pltpu.VMEM((reach, idim), jnp.bfloat16),
                pltpu.VMEM((LANES, idim), jnp.bfloat16),
                pltpu.VMEM((2, heads // 2 * half, LANES), jnp.float32),
                pltpu.VMEM((1, index_heads * half, LANES), jnp.float32),
                pltpu.VMEM((2, min(4, heads // 2) * half, reach), jnp.float32),
                pltpu.SMEM((block_order.shape[0],), jnp.int32),
            ],
            compiler_params=pltpu.CompilerParams(vmem_limit_bytes=28 << 20),
            cost_estimate=pl.CostEstimate(
                flops=2 * half * reach * heads * key_pad, bytes_accessed=4 << 20, transcendentals=0
            ),
            name="keep_sums" if keep else "give_sums",
        )(block_order, segment_ids, bias, near_query, index_query_here, *keys)

    given, key_stack = block_sums(False, pieces)
    kept = block_sums(True, [key_stack])
    value = kept + swap(given, "head", 1)
    distances = [1 << k for k in range(1, n_head.bit_length() - 1)]
    for distance in distances[:-1]:
        value = value + swap(value, "head", distance)
    values = [value] + [swap(value, "head", distance) for distance in distances[-1:]]
    loss = pl.pallas_call(
        functools.partial(loss_kernel, (half, heads * n_head)),
        out_shape=jax.ShapeDtypeStruct((1, rows), jnp.float32),
        in_specs=[vmem] * (1 + len(values)),
        out_specs=vmem,
        compiler_params=pltpu.CompilerParams(vmem_limit_bytes=8 << 20),
        name="row_losses",
    )(bias, *values)
    return (loss + swap(loss, "head", 1)).reshape(rows)


def solution(mesh):
    in_specs = (
        P("ctx", None),
        P("ctx", None),
        P("ctx", "head"),
        P("ctx", "head"),
        P("ctx", "head"),
        P(),
        P(),
    )
    return jax.shard_map(per_device, mesh=mesh, in_specs=in_specs, out_specs=P("ctx"), check_vma=False)
```

```python
import functools
import math

import jax
import jax.numpy as jnp
from jax import lax
from jax.experimental import pallas as pl
from jax.experimental.pallas import tpu as pltpu
from jax.sharding import PartitionSpec as P


LANES = 128
score_scale = 192.0 ** (-0.5)
hidden = -1e30


def swap(x, axis, distance):
    size = lax.axis_size(axis)
    return lax.ppermute(x, axis, [(i, i ^ distance) for i in range(size)])


def window_masks(block, reach, half, seg_ref):
    table_rows = seg_ref.shape[0]
    first = block - reach // half
    row0 = lax.div(first + 2 * table_rows, 2) - table_rows
    pieces = []
    for k in range(reach // LANES + 2):
        row = jnp.clip(row0 + k, 0, table_rows - 1)
        pieces.append(seg_ref[pl.ds(row, 1), :].astype(jnp.float32))
    wide = jnp.concatenate(pieces, axis=1)
    width = wide.shape[1]
    moved = pltpu.roll(wide, width - half, 1)
    odd = lax.rem(first + 2 * table_rows, 2)
    wide = jnp.where(odd == 1, moved, wide)
    tail_seg = jnp.broadcast_to(wide[:, reach : reach + LANES], (half, LANES))
    head_seg = jnp.broadcast_to(wide[:, :LANES], (half, LANES))
    row_id = lax.broadcasted_iota(jnp.int32, (half, LANES), 0)
    lane_id = lax.broadcasted_iota(jnp.int32, (half, LANES), 1)
    query_seg = jnp.sum(jnp.where(row_id == lane_id, tail_seg, 0.0), axis=1, keepdims=True)
    in_tail = (lane_id <= row_id) & (lane_id < half)
    key_seg = jnp.concatenate(
        [jnp.where(in_tail, tail_seg, head_seg), jnp.broadcast_to(wide[:, LANES:reach], (half, reach - LANES))], axis=1
    )
    place = lax.broadcasted_iota(jnp.int32, (half, reach), 1)
    rows_full = lax.broadcasted_iota(jnp.int32, (half, reach), 0)
    tail_full = (place <= rows_full) & (place < half)
    position = first * half + place + jnp.where(tail_full, reach, 0)
    visible = (key_seg == query_seg) & (position >= 0)
    return in_tail, visible


def ring_fold(own_low, main, tail):
    low = jnp.where(own_low, main[:, :LANES], tail)
    return jnp.concatenate([low, main[:, LANES:]], axis=1)


def own_block(keep):
    bit = lax.axis_index("head") & 1
    return bit if keep else 1 - bit


def block_rows(keep, half):
    return pl.ds(pl.multiple_of(own_block(keep) * half, half), half)


def pack_kernel(latent_hbm, index_hbm, out_ref, part_ref, sems):
    width = latent_hbm.shape[0]
    part = part_ref.shape[0]
    bit = own_block(True)
    whole = [
        pltpu.make_async_copy(latent_hbm, out_ref.at[:width, :], sems.at[0]),
        pltpu.make_async_copy(index_hbm, out_ref.at[width:, :], sems.at[1]),
    ]
    low = [pltpu.make_async_copy(latent_hbm.at[:part, :], part_ref, sems.at[2])]
    high = [
        pltpu.make_async_copy(latent_hbm.at[part:, :], part_ref.at[: width - part, :], sems.at[2]),
        pltpu.make_async_copy(index_hbm, part_ref.at[width - part :, :], sems.at[3]),
    ]

    def each(copies, act):
        for copy in copies:
            act(copy)

    for act in (lambda copy: copy.start(), lambda copy: copy.wait()):
        each(whole, act)
        pl.when(bit == 0)(functools.partial(each, low, act))
        pl.when(bit == 1)(functools.partial(each, high, act))


def prelude_kernel(sizes, order_hbm, seg_hbm, weight_hbm, query_hbm, index_query_hbm,
                   bias_ref, query_ref, keep_ref, give_ref, order_ref, seg_ref, weight_ref, sems):
    half, reach, copies = sizes
    rows = query_ref.shape[0]
    width = index_query_hbm.shape[1]
    small = [
        pltpu.make_async_copy(order_hbm, order_ref, sems.at[0]),
        pltpu.make_async_copy(seg_hbm, seg_ref, sems.at[1]),
        pltpu.make_async_copy(weight_hbm, weight_ref, sems.at[2]),
    ]
    large = [
        pltpu.make_async_copy(index_query_hbm.at[block_rows(False, half), :], give_ref.at[:, :width], sems.at[3]),
        pltpu.make_async_copy(index_query_hbm.at[block_rows(True, half), :], keep_ref.at[:, :width], sems.at[4]),
    ]
    for c in range(copies):
        part = slice(c * (rows // copies), (c + 1) * (rows // copies))
        large.append(pltpu.make_async_copy(query_hbm.at[part, :], query_ref.at[part, :], sems.at[5 + c]))
    for copy in small + large:
        copy.start()
    for copy in small:
        copy.wait()
    me = lax.axis_index("ctx")
    for i in range(2):
        _, visible = window_masks(order_ref[me * 2 + i], reach, half, seg_ref)
        bias_ref[i] = jnp.where(visible, 0.0, hidden)
    gains = jnp.transpose(weight_ref[...].astype(jnp.float32), (1, 0))
    gains = jnp.concatenate([gains, jnp.zeros((rows, LANES - gains.shape[1]), gains.dtype)], axis=1)
    gains = gains.astype(keep_ref.dtype)
    first_kept = own_block(True) == 0
    keep_ref[:, width:] = jnp.where(first_kept, gains[:half], gains[half:])
    give_ref[:, width:] = jnp.where(first_kept, gains[half:], gains[:half])
    for copy in large:
        copy.wait()


def block_kernel(sizes, keep, order_ref, seg_ref, bias_ref, query_ref, *refs):
    n_ctx, half, reach, key_width, idim = sizes
    n_index = 2 if keep else 0
    index_query_refs, refs = refs[:n_index], refs[n_index:]
    if keep:
        stack_ref, refs = refs[0], refs[1:]
    else:
        piece_refs, half_refs, refs = refs[: n_ctx - 2], refs[n_ctx - 2 : n_ctx + 2], refs[n_ctx + 2 :]
    out_refs, refs = refs[:2], refs[2:]
    main_ref, tail_ref, index_main, index_tail, raw_ref, index_raw, main_raw, inverse_ref = refs
    key_pad = main_ref.shape[1]
    me = lax.axis_index("ctx")
    mine = own_block(keep)
    rows_here = block_rows(keep, half)
    if not keep:
        stack_ref = out_refs[1]
        bit = own_block(True)
        for s in range(n_ctx - 2):
            stack_ref[me ^ s] = piece_refs[s][...]
        part = stack_ref.shape[1] // 2
        for k, ref in enumerate(half_refs):
            at = pl.multiple_of((bit if k % 2 == 0 else 1 - bit) * part, part)
            stack_ref[me ^ (n_ctx - 2 + k // 2), pl.ds(at, part), :] = ref[...]
    for slot in range(order_ref.shape[0]):
        inverse_ref[order_ref[slot]] = slot
    block = order_ref[me * 2 + mine]
    reach_blocks = reach // half
    first = block - reach_blocks
    oldest = jnp.maximum(first, 0) * half + half - 1
    needed = (first >= 0) & (seg_ref[block * half] == seg_ref[oldest])
    order = [reach_blocks] + list(range(1, reach_blocks)) + [0]
    slots = [inverse_ref[jnp.maximum(first + w, 0)] for w in order]

    left = lax.broadcasted_iota(jnp.int32, (key_width, LANES), 1) < half

    def keys_into(target_ref, c, lanes):
        near, away = [slots[min(2 * c + side, reach_blocks)] for side in (0, 1)]
        first_tile = stack_ref[near >> 1, :key_width, :]
        second_tile = stack_ref[away >> 1, :key_width, :]
        turned = pltpu.roll(jnp.where(left, second_tile, first_tile), half, 1)
        both = jnp.where(
            left, jnp.where((near & 1) == 0, first_tile, turned), jnp.where((away & 1) == 1, second_tile, turned)
        )
        target_ref[0, :key_width, lanes] = both
        target_ref[1, key_pad - key_width :, lanes] = both

    def index_keys_into(target_ref, w, at):
        start = pl.multiple_of(key_width + (slots[w] & 1) * half, half)
        target_ref[at : at + half, :] = stack_ref[slots[w] >> 1, pl.ds(start, half), :]

    main_ref[0, key_width:, :] = jnp.zeros((key_pad - key_width, reach), main_ref.dtype)
    main_ref[1, : key_pad - key_width, :] = jnp.zeros((key_pad - key_width, reach), main_ref.dtype)
    for c in range(reach // LANES):
        keys_into(main_ref, c, slice(c * LANES, (c + 1) * LANES))

    row_id = lax.broadcasted_iota(jnp.int32, (half, LANES), 0)
    lane_id = lax.broadcasted_iota(jnp.int32, (half, LANES), 1)
    own_low = (lane_id <= row_id) | (lane_id >= half) | jnp.logical_not(needed)
    bias = bias_ref[mine]

    heads = query_ref.shape[1] // key_width
    stacked_queries = []
    for parity in (0, 1):
        starts = [g * 2 * key_width + parity * (2 * key_width - key_pad) for g in range(heads // 2)]
        stacked_queries.append(lambda starts=starts: jnp.concatenate([query_ref[rows_here, at : at + key_pad] for at in starts], axis=0))

    def index_lhs(ref):
        return jnp.concatenate([ref[:, j * idim : (j + 1) * idim] for j in range(ref.shape[1] // idim - 1)], axis=0)

    if keep:
        for w in range(reach_blocks):
            index_keys_into(index_main, w, w * half)

    @pl.when(needed)
    def _():
        tail_ref[0, key_width:, :] = jnp.zeros((key_pad - key_width, LANES), tail_ref.dtype)
        tail_ref[1, : key_pad - key_width, :] = jnp.zeros((key_pad - key_width, LANES), tail_ref.dtype)
        keys_into(tail_ref, reach // LANES, slice(0, LANES))
        for parity in (0, 1):
            raw_ref[parity] = lax.dot_general(
                stacked_queries[parity](), tail_ref[parity], (((1,), (0,)), ((), ())), preferred_element_type=jnp.float32
            )
        if keep:
            index_keys_into(index_tail, reach_blocks, 0)
            index_tail[half:, :] = jnp.zeros((LANES - half, idim), index_tail.dtype)
            for k, ref in enumerate(index_query_refs):
                index_raw[k] = lax.dot_general(
                    index_lhs(ref), index_tail[...], (((1,), (1,)), ((), ())), preferred_element_type=jnp.float32
                )

    groups = 2 * max(1, heads // 2 // 4)
    each = heads // groups

    def matmul(k):
        parity = k % 2
        starts = [(g + k // 2 * each) * 2 * key_width + parity * (2 * key_width - key_pad) for g in range(each)]
        lhs = jnp.concatenate([query_ref[rows_here, at : at + key_pad] for at in starts], axis=0)
        main_raw[k % 2] = lax.dot_general(
            lhs, main_ref[parity], (((1,), (0,)), ((), ())), preferred_element_type=jnp.float32
        )

    def softmax(k, total):
        for g in range(each):
            tail = raw_ref[k % 2, (g + k // 2 * each) * half : (g + k // 2 * each + 1) * half, :]
            scores = ring_fold(own_low, main_raw[k % 2, g * half : (g + 1) * half, :], tail) + bias
            row_max = jnp.max(scores, axis=1, keepdims=True)
            powers = jnp.exp2((scores - row_max) * (score_scale * math.log2(math.e)))
            share = 1.0 / jnp.sum(powers, axis=1, keepdims=True)
            total = total + powers * share
        return total

    total = jnp.zeros((half, reach), jnp.float32)
    matmul(0)
    for k in range(1, groups + 1):
        if k < groups:
            matmul(k)
        total = softmax(k - 1, total)
    out_refs[0][...] = total

    if keep:
        total = jnp.zeros((half, reach), jnp.float32)
        for k, ref in enumerate(index_query_refs):
            lhs = index_lhs(ref)
            dots = lax.dot_general(lhs, index_main[...], (((1,), (1,)), ((), ())), preferred_element_type=jnp.float32)
            gains = ref[:, lhs.shape[0] // half * idim :].astype(jnp.float32)
            for j in range(lhs.shape[0] // half):
                here = slice(j * half, (j + 1) * half)
                folded = ring_fold(own_low, dots[here, :], index_raw[k, here, :])
                total = total + gains[:, j : j + 1] * jnp.maximum(folded, 0.0)
        out_refs[1][...] = jnp.where(bias == 0.0, total, 0.0)


def loss_kernel(sizes, bias_ref, *refs):
    half, total_heads, across = sizes
    value_refs, out_ref = refs[:-1], refs[-1]
    mine = own_block(True)
    visible = bias_ref[mine] == 0.0
    target = functools.reduce(jnp.add, [ref[0] for ref in value_refs]) * (1.0 / total_heads)
    index_score = functools.reduce(jnp.add, [ref[1] for ref in value_refs])
    masked = jnp.where(visible, index_score, hidden)
    row_max = jnp.max(masked, axis=1, keepdims=True)
    exp_sum = jnp.sum(jnp.where(visible, jnp.exp(masked - row_max), 0.0), axis=1, keepdims=True)
    positive = target > 0.0
    logs = jnp.log(jnp.where(positive, target, 1.0))
    entropy_sum = jnp.sum(jnp.where(positive, target * logs, 0.0), axis=1, keepdims=True)
    cross_sum = jnp.sum(jnp.where(visible, target * index_score, 0.0), axis=1, keepdims=True)
    target_sum = jnp.sum(target, axis=1, keepdims=True)
    column = entropy_sum - cross_sum + (row_max + jnp.log(exp_sum)) * target_sum
    rows = out_ref.shape[1]
    row_id = lax.broadcasted_iota(jnp.int32, (half, rows), 0)
    lane_id = lax.broadcasted_iota(jnp.int32, (half, rows), 1)
    owner = mine != (lax.axis_index("head") // across) & 1
    place = (row_id + mine * half == lane_id) & owner
    out_ref[...] = jnp.sum(jnp.where(place, column, 0.0), axis=0, keepdims=True)


def per_device(
    latent_keys, index_keys, main_query, index_query, index_weight, segment_ids, block_order
):
    n_ctx, n_head = lax.axis_size("ctx"), lax.axis_size("head")
    rows, key_width = latent_keys.shape
    idim = index_keys.shape[1]
    seq_len = segment_ids.shape[0]
    half = seq_len // block_order.shape[0]
    reach = seq_len // 4
    heads = main_query.shape[1] // key_width
    key_pad = -(-key_width // LANES) * LANES
    vmem = pl.BlockSpec(memory_space=pltpu.VMEM)
    smem = pl.BlockSpec(memory_space=pltpu.SMEM)
    hbm = pl.BlockSpec(memory_space=pltpu.HBM)
    index_heads = index_weight.shape[1]

    def far(x):
        return pltpu.with_memory_space_constraint(x, pltpu.HBM)

    packed, part = pl.pallas_call(
        pack_kernel,
        out_shape=(
            jax.ShapeDtypeStruct((key_width + idim, rows), latent_keys.dtype),
            jax.ShapeDtypeStruct(((key_width + idim) // 2, rows), latent_keys.dtype),
        ),
        in_specs=[hbm, hbm],
        out_specs=(vmem, vmem),
        scratch_shapes=[pltpu.SemaphoreType.DMA((4,))],
        compiler_params=pltpu.CompilerParams(vmem_limit_bytes=2 << 20),
        name="pack",
    )(far(latent_keys.T), far(index_keys))
    last = n_ctx // 2 - 1
    corner = swap(part, "ctx", 2 * last)
    own_core = []
    for s in reversed(range(1, last)):
        own_core.append(swap(packed, "ctx", 2 * s))
    corner_rest = swap(corner, "head", 1)
    pieces = []
    for piece in [packed] + own_core[::-1]:
        pieces += [piece, swap(piece, "ctx", 1)]
    pieces += [corner, corner_rest, swap(corner, "ctx", 1), swap(corner_rest, "ctx", 1)]
    seg_table = segment_ids.reshape(seq_len // LANES, LANES)

    copies = 8
    index_row = (half, index_query.shape[1] + LANES)
    bias, near_query, keep_query, give_query = pl.pallas_call(
        functools.partial(prelude_kernel, (half, reach, copies)),
        out_shape=(
            jax.ShapeDtypeStruct((2, half, reach), jnp.float32),
            jax.ShapeDtypeStruct(main_query.shape, main_query.dtype),
            jax.ShapeDtypeStruct(index_row, index_query.dtype),
            jax.ShapeDtypeStruct(index_row, index_query.dtype),
        ),
        in_specs=[hbm] * 5,
        out_specs=(vmem,) * 4,
        scratch_shapes=[
            pltpu.SMEM(block_order.shape, jnp.int32),
            pltpu.VMEM(seg_table.shape, jnp.int32),
            pltpu.VMEM((index_heads, rows), index_weight.dtype),
            pltpu.SemaphoreType.DMA((copies + 5,)),
        ],
        compiler_params=pltpu.CompilerParams(vmem_limit_bytes=12 << 20),
        cost_estimate=pl.CostEstimate(flops=1 << 20, bytes_accessed=10 << 20, transcendentals=0),
        name="prelude",
    )(far(block_order), far(seg_table), far(index_weight.T), far(main_query), far(index_query))
    taken_query = swap(give_query, "head", 1)

    stack = jax.ShapeDtypeStruct((n_ctx, key_width + idim, rows), packed.dtype)

    def block_sums(keep, keys):
        sums = jax.ShapeDtypeStruct((half, reach), jnp.float32)
        index_queries = [keep_query, taken_query] if keep else []
        return pl.pallas_call(
            functools.partial(block_kernel, (n_ctx, half, reach, key_width, idim), keep),
            out_shape=(sums, sums) if keep else (sums, stack),
            in_specs=[smem, smem] + [vmem] * (2 + len(index_queries) + len(keys)),
            out_specs=(vmem, vmem),
            scratch_shapes=[
                pltpu.VMEM((2, key_pad, reach), jnp.bfloat16),
                pltpu.VMEM((2, key_pad, LANES), jnp.bfloat16),
                pltpu.VMEM((reach, idim), jnp.bfloat16),
                pltpu.VMEM((LANES, idim), jnp.bfloat16),
                pltpu.VMEM((2, heads // 2 * half, LANES), jnp.float32),
                pltpu.VMEM((2, index_heads * half, LANES), jnp.float32),
                pltpu.VMEM((2, min(4, heads // 2) * half, reach), jnp.float32),
                pltpu.SMEM((block_order.shape[0],), jnp.int32),
            ],
            compiler_params=pltpu.CompilerParams(vmem_limit_bytes=28 << 20),
            cost_estimate=pl.CostEstimate(
                flops=2 * half * reach * heads * key_pad, bytes_accessed=4 << 20, transcendentals=0
            ),
            name="keep_sums" if keep else "give_sums",
        )(block_order, segment_ids, bias, near_query, *index_queries, *keys)

    given, key_stack = block_sums(False, pieces)
    kept, index_sums = block_sums(True, [key_stack])
    value = jnp.stack([kept + swap(given, "head", 1), index_sums])
    distances = [1 << k for k in range(1, n_head.bit_length() - 1)]
    for distance in distances[:-1]:
        value = value + swap(value, "head", distance)
    across = distances[-1]
    owners = [i for i in range(n_head) if i & 1 != (i // across) & 1]
    values = [value, lax.ppermute(value, "head", [(i ^ across, i) for i in owners])]
    loss = pl.pallas_call(
        functools.partial(loss_kernel, (half, heads * n_head, across)),
        out_shape=jax.ShapeDtypeStruct((1, rows), jnp.float32),
        in_specs=[vmem] * (1 + len(values)),
        out_specs=vmem,
        compiler_params=pltpu.CompilerParams(vmem_limit_bytes=8 << 20),
        name="row_losses",
    )(bias, *values)
    loss = loss + lax.ppermute(loss, "head", [(i, i ^ across ^ 1) for i in owners])
    return (loss + lax.ppermute(loss, "head", [(i, i ^ 1) for i in owners])).reshape(rows)


def solution(mesh):
    in_specs = (
        P("ctx", None),
        P("ctx", None),
        P("ctx", "head"),
        P("ctx", "head"),
        P("ctx", "head"),
        P(),
        P(),
    )
    return jax.shard_map(per_device, mesh=mesh, in_specs=in_specs, out_specs=P("ctx"), check_vma=False)
```

```python
import functools
import math

import jax
import jax.numpy as jnp
from jax import lax
from jax.experimental import pallas as pl
from jax.experimental.pallas import tpu as pltpu
from jax.sharding import PartitionSpec as P


LANES = 128
score_scale = 192.0 ** (-0.5)
hidden = -1e30


def swap(x, axis, distance):
    size = lax.axis_size(axis)
    return lax.ppermute(x, axis, [(i, i ^ distance) for i in range(size)])


def window_masks(block, reach, half, seg_ref):
    table_rows = seg_ref.shape[0]
    first = block - reach // half
    row0 = lax.div(first + 2 * table_rows, 2) - table_rows
    pieces = []
    for k in range(reach // LANES + 2):
        row = jnp.clip(row0 + k, 0, table_rows - 1)
        pieces.append(seg_ref[pl.ds(row, 1), :].astype(jnp.float32))
    wide = jnp.concatenate(pieces, axis=1)
    width = wide.shape[1]
    moved = pltpu.roll(wide, width - half, 1)
    odd = lax.rem(first + 2 * table_rows, 2)
    wide = jnp.where(odd == 1, moved, wide)
    tail_seg = jnp.broadcast_to(wide[:, reach : reach + LANES], (half, LANES))
    head_seg = jnp.broadcast_to(wide[:, :LANES], (half, LANES))
    row_id = lax.broadcasted_iota(jnp.int32, (half, LANES), 0)
    lane_id = lax.broadcasted_iota(jnp.int32, (half, LANES), 1)
    query_seg = jnp.sum(jnp.where(row_id == lane_id, tail_seg, 0.0), axis=1, keepdims=True)
    in_tail = (lane_id <= row_id) & (lane_id < half)
    key_seg = jnp.concatenate(
        [jnp.where(in_tail, tail_seg, head_seg), jnp.broadcast_to(wide[:, LANES:reach], (half, reach - LANES))], axis=1
    )
    place = lax.broadcasted_iota(jnp.int32, (half, reach), 1)
    rows_full = lax.broadcasted_iota(jnp.int32, (half, reach), 0)
    tail_full = (place <= rows_full) & (place < half)
    position = first * half + place + jnp.where(tail_full, reach, 0)
    visible = (key_seg == query_seg) & (position >= 0)
    return in_tail, visible


def ring_fold(own_low, main, tail):
    low = jnp.where(own_low, main[:, :LANES], tail)
    return jnp.concatenate([low, main[:, LANES:]], axis=1)


def own_block(keep):
    bit = lax.axis_index("head") & 1
    return bit if keep else 1 - bit


def block_rows(keep, half):
    return pl.ds(pl.multiple_of(own_block(keep) * half, half), half)


def pack_kernel(latent_hbm, index_hbm, out_ref, part_ref, sems):
    width = latent_hbm.shape[0]
    part = part_ref.shape[0]
    bit = own_block(True)
    whole = [
        pltpu.make_async_copy(latent_hbm, out_ref.at[:width, :], sems.at[0]),
        pltpu.make_async_copy(index_hbm, out_ref.at[width:, :], sems.at[1]),
    ]
    low = [pltpu.make_async_copy(latent_hbm.at[:part, :], part_ref, sems.at[2])]
    high = [
        pltpu.make_async_copy(latent_hbm.at[part:, :], part_ref.at[: width - part, :], sems.at[2]),
        pltpu.make_async_copy(index_hbm, part_ref.at[width - part :, :], sems.at[3]),
    ]

    def each(copies, act):
        for copy in copies:
            act(copy)

    for act in (lambda copy: copy.start(), lambda copy: copy.wait()):
        each(whole, act)
        pl.when(bit == 0)(functools.partial(each, low, act))
        pl.when(bit == 1)(functools.partial(each, high, act))


def prelude_kernel(sizes, order_hbm, seg_hbm, weight_hbm, query_hbm, index_query_hbm,
                   bias_ref, query_ref, keep_ref, give_ref, order_ref, seg_ref, weight_ref, sems):
    half, reach, copies = sizes
    rows = query_ref.shape[0]
    width = index_query_hbm.shape[1]
    small = [
        pltpu.make_async_copy(order_hbm, order_ref, sems.at[0]),
        pltpu.make_async_copy(seg_hbm, seg_ref, sems.at[1]),
        pltpu.make_async_copy(weight_hbm, weight_ref, sems.at[2]),
    ]
    large = [
        pltpu.make_async_copy(index_query_hbm.at[block_rows(False, half), :], give_ref.at[:, :width], sems.at[3]),
        pltpu.make_async_copy(index_query_hbm.at[block_rows(True, half), :], keep_ref.at[:, :width], sems.at[4]),
    ]
    for c in range(copies):
        part = slice(c * (rows // copies), (c + 1) * (rows // copies))
        large.append(pltpu.make_async_copy(query_hbm.at[part, :], query_ref.at[part, :], sems.at[5 + c]))
    for copy in small + large:
        copy.start()
    for copy in small:
        copy.wait()
    me = lax.axis_index("ctx")
    for i in range(2):
        _, visible = window_masks(order_ref[me * 2 + i], reach, half, seg_ref)
        bias_ref[i] = jnp.where(visible, 0.0, hidden)
    gains = jnp.transpose(weight_ref[...].astype(jnp.float32), (1, 0))
    gains = jnp.concatenate([gains, jnp.zeros((rows, LANES - gains.shape[1]), gains.dtype)], axis=1)
    gains = gains.astype(keep_ref.dtype)
    first_kept = own_block(True) == 0
    keep_ref[:, width:] = jnp.where(first_kept, gains[:half], gains[half:])
    give_ref[:, width:] = jnp.where(first_kept, gains[half:], gains[:half])
    for copy in large:
        copy.wait()


def block_kernel(sizes, keep, order_ref, seg_ref, bias_ref, query_ref, *refs):
    n_ctx, half, reach, key_width, idim = sizes
    n_index = 2 if keep else 0
    index_query_refs, refs = refs[:n_index], refs[n_index:]
    if keep:
        stack_ref, refs = refs[0], refs[1:]
    else:
        piece_refs, half_refs, refs = refs[: n_ctx - 2], refs[n_ctx - 2 : n_ctx + 2], refs[n_ctx + 2 :]
    out_refs, refs = refs[:2], refs[2:]
    main_ref, tail_ref, index_main, index_tail, raw_ref, index_raw, main_raw, inverse_ref = refs
    key_pad = main_ref.shape[1]
    me = lax.axis_index("ctx")
    mine = own_block(keep)
    rows_here = block_rows(keep, half)
    if not keep:
        stack_ref = out_refs[1]
        bit = own_block(True)
        for s in range(n_ctx - 2):
            stack_ref[me ^ s] = piece_refs[s][...]
        part = stack_ref.shape[1] // 2
        for k, ref in enumerate(half_refs):
            at = pl.multiple_of((bit if k % 2 == 0 else 1 - bit) * part, part)
            stack_ref[me ^ (n_ctx - 2 + k // 2), pl.ds(at, part), :] = ref[...]
    for slot in range(order_ref.shape[0]):
        inverse_ref[order_ref[slot]] = slot
    block = order_ref[me * 2 + mine]
    reach_blocks = reach // half
    first = block - reach_blocks
    oldest = jnp.maximum(first, 0) * half + half - 1
    needed = (first >= 0) & (seg_ref[block * half] == seg_ref[oldest])
    order = [reach_blocks] + list(range(1, reach_blocks)) + [0]
    slots = [inverse_ref[jnp.maximum(first + w, 0)] for w in order]

    left = lax.broadcasted_iota(jnp.int32, (key_width, LANES), 1) < half

    def keys_into(target_ref, c, lanes):
        near, away = [slots[min(2 * c + side, reach_blocks)] for side in (0, 1)]
        first_tile = stack_ref[near >> 1, :key_width, :]
        second_tile = stack_ref[away >> 1, :key_width, :]
        turned = pltpu.roll(jnp.where(left, second_tile, first_tile), half, 1)
        both = jnp.where(
            left, jnp.where((near & 1) == 0, first_tile, turned), jnp.where((away & 1) == 1, second_tile, turned)
        )
        target_ref[0, :key_width, lanes] = both
        target_ref[1, key_pad - key_width :, lanes] = both

    def index_keys_into(target_ref, w, at):
        start = pl.multiple_of(key_width + (slots[w] & 1) * half, half)
        target_ref[at : at + half, :] = stack_ref[slots[w] >> 1, pl.ds(start, half), :]

    main_ref[0, key_width:, :] = jnp.zeros((key_pad - key_width, reach), main_ref.dtype)
    main_ref[1, : key_pad - key_width, :] = jnp.zeros((key_pad - key_width, reach), main_ref.dtype)
    for c in range(reach // LANES):
        keys_into(main_ref, c, slice(c * LANES, (c + 1) * LANES))

    row_id = lax.broadcasted_iota(jnp.int32, (half, LANES), 0)
    lane_id = lax.broadcasted_iota(jnp.int32, (half, LANES), 1)
    own_low = (lane_id <= row_id) | (lane_id >= half) | jnp.logical_not(needed)
    bias = bias_ref[mine]

    heads = query_ref.shape[1] // key_width
    stacked_queries = []
    for parity in (0, 1):
        starts = [g * 2 * key_width + parity * (2 * key_width - key_pad) for g in range(heads // 2)]
        stacked_queries.append(lambda starts=starts: jnp.concatenate([query_ref[rows_here, at : at + key_pad] for at in starts], axis=0))

    def index_lhs(ref):
        return jnp.concatenate([ref[:, j * idim : (j + 1) * idim] for j in range(ref.shape[1] // idim - 1)], axis=0)

    if keep:
        for w in range(reach_blocks):
            index_keys_into(index_main, w, w * half)

    @pl.when(needed)
    def _():
        tail_ref[0, key_width:, :] = jnp.zeros((key_pad - key_width, LANES), tail_ref.dtype)
        tail_ref[1, : key_pad - key_width, :] = jnp.zeros((key_pad - key_width, LANES), tail_ref.dtype)
        keys_into(tail_ref, reach // LANES, slice(0, LANES))
        for parity in (0, 1):
            raw_ref[parity] = lax.dot_general(
                stacked_queries[parity](), tail_ref[parity], (((1,), (0,)), ((), ())), preferred_element_type=jnp.float32
            )
        if keep:
            index_keys_into(index_tail, reach_blocks, 0)
            index_tail[half:, :] = jnp.zeros((LANES - half, idim), index_tail.dtype)
            for k, ref in enumerate(index_query_refs):
                index_raw[k] = lax.dot_general(
                    index_lhs(ref), index_tail[...], (((1,), (1,)), ((), ())), preferred_element_type=jnp.float32
                )

    groups = 2 * max(1, heads // 2 // 4)
    each = heads // groups

    def matmul(k):
        parity = k % 2
        starts = [(g + k // 2 * each) * 2 * key_width + parity * (2 * key_width - key_pad) for g in range(each)]
        lhs = jnp.concatenate([query_ref[rows_here, at : at + key_pad] for at in starts], axis=0)
        main_raw[k % 2] = lax.dot_general(
            lhs, main_ref[parity], (((1,), (0,)), ((), ())), preferred_element_type=jnp.float32
        )

    def softmax(k, total):
        for g in range(each):
            tail = raw_ref[k % 2, (g + k // 2 * each) * half : (g + k // 2 * each + 1) * half, :]
            scores = ring_fold(own_low, main_raw[k % 2, g * half : (g + 1) * half, :], tail) + bias
            row_max = jnp.max(scores, axis=1, keepdims=True)
            powers = jnp.exp2((scores - row_max) * (score_scale * math.log2(math.e)))
            share = 1.0 / jnp.sum(powers, axis=1, keepdims=True)
            total = total + powers * share
        return total

    total = jnp.zeros((half, reach), jnp.float32)
    matmul(0)
    for k in range(1, groups + 1):
        if k < groups:
            matmul(k)
        total = softmax(k - 1, total)
    out_refs[0][...] = total

    if keep:
        total = jnp.zeros((half, reach), jnp.float32)
        for k, ref in enumerate(index_query_refs):
            lhs = index_lhs(ref)
            dots = lax.dot_general(lhs, index_main[...], (((1,), (1,)), ((), ())), preferred_element_type=jnp.float32)
            gains = ref[:, lhs.shape[0] // half * idim :].astype(jnp.float32)
            for j in range(lhs.shape[0] // half):
                here = slice(j * half, (j + 1) * half)
                folded = ring_fold(own_low, dots[here, :], index_raw[k, here, :])
                total = total + gains[:, j : j + 1] * jnp.maximum(folded, 0.0)
        out_refs[1][...] = jnp.where(bias == 0.0, total, 0.0)


def split_kernel(across, kept_ref, taken_ref, index_ref, value_ref, rest_ref):
    count = value_ref.shape[1]
    side = (lax.axis_index("head") // across) & 1
    for at, ref in ((side, value_ref), (1 - side, rest_ref)):
        here = pl.ds(pl.multiple_of(at * count, count), count)
        ref[0] = kept_ref[here, :] + taken_ref[here, :]
        ref[1] = index_ref[here, :]


def loss_kernel(sizes, bias_ref, *refs):
    half, total_heads, across = sizes
    value_refs, out_ref = refs[:-1], refs[-1]
    mine = own_block(True)
    count = value_refs[0].shape[1]
    start = ((lax.axis_index("head") // across) & 1) * count
    visible = bias_ref[mine, pl.ds(pl.multiple_of(start, count), count), :] == 0.0
    target = functools.reduce(jnp.add, [ref[0] for ref in value_refs]) * (1.0 / total_heads)
    index_score = functools.reduce(jnp.add, [ref[1] for ref in value_refs])
    masked = jnp.where(visible, index_score, hidden)
    row_max = jnp.max(masked, axis=1, keepdims=True)
    exp_sum = jnp.sum(jnp.where(visible, jnp.exp(masked - row_max), 0.0), axis=1, keepdims=True)
    positive = target > 0.0
    logs = jnp.log(jnp.where(positive, target, 1.0))
    entropy_sum = jnp.sum(jnp.where(positive, target * logs, 0.0), axis=1, keepdims=True)
    cross_sum = jnp.sum(jnp.where(visible, target * index_score, 0.0), axis=1, keepdims=True)
    target_sum = jnp.sum(target, axis=1, keepdims=True)
    column = entropy_sum - cross_sum + (row_max + jnp.log(exp_sum)) * target_sum
    rows = out_ref.shape[1]
    row_id = lax.broadcasted_iota(jnp.int32, (count, rows), 0)
    lane_id = lax.broadcasted_iota(jnp.int32, (count, rows), 1)
    place = row_id + mine * half + start == lane_id
    out_ref[...] = jnp.sum(jnp.where(place, column, 0.0), axis=0, keepdims=True)


def per_device(
    latent_keys, index_keys, main_query, index_query, index_weight, segment_ids, block_order
):
    n_ctx, n_head = lax.axis_size("ctx"), lax.axis_size("head")
    rows, key_width = latent_keys.shape
    idim = index_keys.shape[1]
    seq_len = segment_ids.shape[0]
    half = seq_len // block_order.shape[0]
    reach = seq_len // 4
    heads = main_query.shape[1] // key_width
    key_pad = -(-key_width // LANES) * LANES
    vmem = pl.BlockSpec(memory_space=pltpu.VMEM)
    smem = pl.BlockSpec(memory_space=pltpu.SMEM)
    hbm = pl.BlockSpec(memory_space=pltpu.HBM)
    index_heads = index_weight.shape[1]

    def far(x):
        return pltpu.with_memory_space_constraint(x, pltpu.HBM)

    packed, part = pl.pallas_call(
        pack_kernel,
        out_shape=(
            jax.ShapeDtypeStruct((key_width + idim, rows), latent_keys.dtype),
            jax.ShapeDtypeStruct(((key_width + idim) // 2, rows), latent_keys.dtype),
        ),
        in_specs=[hbm, hbm],
        out_specs=(vmem, vmem),
        scratch_shapes=[pltpu.SemaphoreType.DMA((4,))],
        compiler_params=pltpu.CompilerParams(vmem_limit_bytes=2 << 20),
        name="pack",
    )(far(latent_keys.T), far(index_keys))
    last = n_ctx // 2 - 1
    corner = swap(part, "ctx", 2 * last)
    own_core = []
    for s in reversed(range(1, last)):
        own_core.append(swap(packed, "ctx", 2 * s))
    corner_rest = swap(corner, "head", 1)
    pieces = []
    for piece in [packed] + own_core[::-1]:
        pieces += [piece, swap(piece, "ctx", 1)]
    pieces += [corner, corner_rest, swap(corner, "ctx", 1), swap(corner_rest, "ctx", 1)]
    seg_table = segment_ids.reshape(seq_len // LANES, LANES)

    copies = 8
    index_row = (half, index_query.shape[1] + LANES)
    bias, near_query, keep_query, give_query = pl.pallas_call(
        functools.partial(prelude_kernel, (half, reach, copies)),
        out_shape=(
            jax.ShapeDtypeStruct((2, half, reach), jnp.float32),
            jax.ShapeDtypeStruct(main_query.shape, main_query.dtype),
            jax.ShapeDtypeStruct(index_row, index_query.dtype),
            jax.ShapeDtypeStruct(index_row, index_query.dtype),
        ),
        in_specs=[hbm] * 5,
        out_specs=(vmem,) * 4,
        scratch_shapes=[
            pltpu.SMEM(block_order.shape, jnp.int32),
            pltpu.VMEM(seg_table.shape, jnp.int32),
            pltpu.VMEM((index_heads, rows), index_weight.dtype),
            pltpu.SemaphoreType.DMA((copies + 5,)),
        ],
        compiler_params=pltpu.CompilerParams(vmem_limit_bytes=12 << 20),
        cost_estimate=pl.CostEstimate(flops=1 << 20, bytes_accessed=10 << 20, transcendentals=0),
        name="prelude",
    )(far(block_order), far(seg_table), far(index_weight.T), far(main_query), far(index_query))
    taken_query = swap(give_query, "head", 1)

    stack = jax.ShapeDtypeStruct((n_ctx, key_width + idim, rows), packed.dtype)

    def block_sums(keep, keys):
        sums = jax.ShapeDtypeStruct((half, reach), jnp.float32)
        index_queries = [keep_query, taken_query] if keep else []
        return pl.pallas_call(
            functools.partial(block_kernel, (n_ctx, half, reach, key_width, idim), keep),
            out_shape=(sums, sums) if keep else (sums, stack),
            in_specs=[smem, smem] + [vmem] * (2 + len(index_queries) + len(keys)),
            out_specs=(vmem, vmem),
            scratch_shapes=[
                pltpu.VMEM((2, key_pad, reach), jnp.bfloat16),
                pltpu.VMEM((2, key_pad, LANES), jnp.bfloat16),
                pltpu.VMEM((reach, idim), jnp.bfloat16),
                pltpu.VMEM((LANES, idim), jnp.bfloat16),
                pltpu.VMEM((2, heads // 2 * half, LANES), jnp.float32),
                pltpu.VMEM((2, index_heads * half, LANES), jnp.float32),
                pltpu.VMEM((2, min(4, heads // 2) * half, reach), jnp.float32),
                pltpu.SMEM((block_order.shape[0],), jnp.int32),
            ],
            compiler_params=pltpu.CompilerParams(vmem_limit_bytes=28 << 20),
            cost_estimate=pl.CostEstimate(
                flops=2 * half * reach * heads * key_pad, bytes_accessed=4 << 20, transcendentals=0
            ),
            name="keep_sums" if keep else "give_sums",
        )(block_order, segment_ids, bias, near_query, *index_queries, *keys)

    given, key_stack = block_sums(False, pieces)
    kept, index_sums = block_sums(True, [key_stack])
    across = n_head // 2
    quarter = jax.ShapeDtypeStruct((2, half // 2, reach), jnp.float32)
    value, rest = pl.pallas_call(
        functools.partial(split_kernel, across),
        out_shape=(quarter, quarter),
        in_specs=[vmem] * 3,
        out_specs=(vmem, vmem),
        compiler_params=pltpu.CompilerParams(vmem_limit_bytes=16 << 20),
        name="split_rows",
    )(kept, swap(given, "head", 1), index_sums)
    distance = 2
    while distance < across:
        value = value + swap(value, "head", distance)
        rest = rest + swap(rest, "head", distance)
        distance *= 2
    values = [value, swap(rest, "head", across)]
    loss = pl.pallas_call(
        functools.partial(loss_kernel, (half, heads * n_head, across)),
        out_shape=jax.ShapeDtypeStruct((1, rows), jnp.float32),
        in_specs=[vmem] * (1 + len(values)),
        out_specs=vmem,
        compiler_params=pltpu.CompilerParams(vmem_limit_bytes=8 << 20),
        name="row_losses",
    )(bias, *values)
    loss = loss + swap(loss, "head", across)
    return (loss + swap(loss, "head", 1)).reshape(rows)


def solution(mesh):
    in_specs = (
        P("ctx", None),
        P("ctx", None),
        P("ctx", "head"),
        P("ctx", "head"),
        P("ctx", "head"),
        P(),
        P(),
    )
    return jax.shard_map(per_device, mesh=mesh, in_specs=in_specs, out_specs=P("ctx"), check_vma=False)
```

```python
import functools
import math

import jax
import jax.numpy as jnp
from jax import lax
from jax.experimental import pallas as pl
from jax.experimental.pallas import tpu as pltpu
from jax.sharding import PartitionSpec as P


LANES = 128
score_scale = 192.0 ** (-0.5)
hidden = -1e30


def swap(x, axis, distance):
    size = lax.axis_size(axis)
    return lax.ppermute(x, axis, [(i, i ^ distance) for i in range(size)])


def window_masks(block, reach, half, seg_ref):
    table_rows = seg_ref.shape[0]
    first = block - reach // half
    row0 = lax.div(first + 2 * table_rows, 2) - table_rows
    pieces = []
    for k in range(reach // LANES + 2):
        row = jnp.clip(row0 + k, 0, table_rows - 1)
        pieces.append(seg_ref[pl.ds(row, 1), :].astype(jnp.float32))
    wide = jnp.concatenate(pieces, axis=1)
    width = wide.shape[1]
    moved = pltpu.roll(wide, width - half, 1)
    odd = lax.rem(first + 2 * table_rows, 2)
    wide = jnp.where(odd == 1, moved, wide)
    tail_seg = jnp.broadcast_to(wide[:, reach : reach + LANES], (half, LANES))
    head_seg = jnp.broadcast_to(wide[:, :LANES], (half, LANES))
    row_id = lax.broadcasted_iota(jnp.int32, (half, LANES), 0)
    lane_id = lax.broadcasted_iota(jnp.int32, (half, LANES), 1)
    query_seg = jnp.sum(jnp.where(row_id == lane_id, tail_seg, 0.0), axis=1, keepdims=True)
    in_tail = (lane_id <= row_id) & (lane_id < half)
    key_seg = jnp.concatenate(
        [jnp.where(in_tail, tail_seg, head_seg), jnp.broadcast_to(wide[:, LANES:reach], (half, reach - LANES))], axis=1
    )
    place = lax.broadcasted_iota(jnp.int32, (half, reach), 1)
    rows_full = lax.broadcasted_iota(jnp.int32, (half, reach), 0)
    tail_full = (place <= rows_full) & (place < half)
    position = first * half + place + jnp.where(tail_full, reach, 0)
    visible = (key_seg == query_seg) & (position >= 0)
    return in_tail, visible


def ring_fold(own_low, main, tail):
    low = jnp.where(own_low, main[:, :LANES], tail)
    return jnp.concatenate([low, main[:, LANES:]], axis=1)


def own_block(keep):
    bit = lax.axis_index("head") & 1
    return bit if keep else 1 - bit


def block_rows(keep, half):
    return pl.ds(pl.multiple_of(own_block(keep) * half, half), half)


def run_copies(copies):
    for copy in copies:
        copy.start()
    for copy in copies:
        copy.wait()


def part_kernel(latent_hbm, index_hbm, part_ref, sems):
    width = latent_hbm.shape[0]
    part = part_ref.shape[0]
    middle = part // 2
    low = [(latent_hbm.at[:middle, :], part_ref.at[:middle, :]), (latent_hbm.at[middle:part, :], part_ref.at[middle:, :])]
    high = [
        (latent_hbm.at[part:, :], part_ref.at[: width - part, :]),
        (index_hbm, part_ref.at[width - part :, :]),
    ]
    for bit, pairs in enumerate((low, high)):
        copies = [pltpu.make_async_copy(source, target, sems.at[k]) for k, (source, target) in enumerate(pairs)]
        pl.when(own_block(True) == bit)(functools.partial(run_copies, copies))


def pack_kernel(latent_hbm, index_hbm, out_ref, sems):
    width = latent_hbm.shape[0]
    run_copies([
        pltpu.make_async_copy(latent_hbm, out_ref.at[:width, :], sems.at[0]),
        pltpu.make_async_copy(index_hbm, out_ref.at[width:, :], sems.at[1]),
    ])


def load_kernel(query_hbm, query_ref, sems):
    copies = sems.shape[0]
    each = query_ref.shape[0] // copies
    run_copies([
        pltpu.make_async_copy(query_hbm.at[c * each : (c + 1) * each, :], query_ref.at[c * each : (c + 1) * each, :], sems.at[c])
        for c in range(copies)
    ])


def prelude_kernel(sizes, order_hbm, seg_hbm, weight_hbm, index_query_hbm,
                   bias_ref, keep_ref, give_ref, order_ref, seg_ref, weight_ref, sems):
    half, reach = sizes
    rows = weight_ref.shape[1]
    width = index_query_hbm.shape[1]
    small = [
        pltpu.make_async_copy(order_hbm, order_ref, sems.at[0]),
        pltpu.make_async_copy(seg_hbm, seg_ref, sems.at[1]),
        pltpu.make_async_copy(weight_hbm, weight_ref, sems.at[2]),
    ]
    large = [
        pltpu.make_async_copy(index_query_hbm.at[block_rows(False, half), :], give_ref.at[:, :width], sems.at[3]),
        pltpu.make_async_copy(index_query_hbm.at[block_rows(True, half), :], keep_ref.at[:, :width], sems.at[4]),
    ]
    for copy in small + large:
        copy.start()
    for copy in small:
        copy.wait()
    me = lax.axis_index("ctx")
    for i in range(2):
        _, visible = window_masks(order_ref[me * 2 + i], reach, half, seg_ref)
        bias_ref[i] = jnp.where(visible, 0.0, hidden)
    gains = jnp.transpose(weight_ref[...].astype(jnp.float32), (1, 0))
    gains = jnp.concatenate([gains, jnp.zeros((rows, LANES - gains.shape[1]), gains.dtype)], axis=1)
    gains = gains.astype(keep_ref.dtype)
    first_kept = own_block(True) == 0
    keep_ref[:, width:] = jnp.where(first_kept, gains[:half], gains[half:])
    give_ref[:, width:] = jnp.where(first_kept, gains[half:], gains[:half])
    for copy in large:
        copy.wait()


def block_kernel(sizes, keep, order_ref, seg_ref, bias_ref, query_ref, *refs):
    n_ctx, half, reach, key_width, idim = sizes
    n_index = 2 if keep else 0
    index_query_refs, refs = refs[:n_index], refs[n_index:]
    if keep:
        stack_ref, refs = refs[0], refs[1:]
    else:
        piece_refs, half_refs, refs = refs[: n_ctx - 2], refs[n_ctx - 2 : n_ctx + 2], refs[n_ctx + 2 :]
    out_refs, refs = refs[:2], refs[2:]
    main_ref, tail_ref, index_main, index_tail, raw_ref, index_raw, main_raw, inverse_ref = refs
    key_pad = main_ref.shape[1]
    me = lax.axis_index("ctx")
    mine = own_block(keep)
    rows_here = block_rows(keep, half)
    if not keep:
        stack_ref = out_refs[1]
        bit = own_block(True)
        for s in range(n_ctx - 2):
            stack_ref[me ^ s] = piece_refs[s][...]
        part = stack_ref.shape[1] // 2
        for k, ref in enumerate(half_refs):
            at = pl.multiple_of((bit if k % 2 == 0 else 1 - bit) * part, part)
            stack_ref[me ^ (n_ctx - 2 + k // 2), pl.ds(at, part), :] = ref[...]
    for slot in range(order_ref.shape[0]):
        inverse_ref[order_ref[slot]] = slot
    block = order_ref[me * 2 + mine]
    reach_blocks = reach // half
    first = block - reach_blocks
    oldest = jnp.maximum(first, 0) * half + half - 1
    needed = (first >= 0) & (seg_ref[block * half] == seg_ref[oldest])
    order = [reach_blocks] + list(range(1, reach_blocks)) + [0]
    slots = [inverse_ref[jnp.maximum(first + w, 0)] for w in order]

    left = lax.broadcasted_iota(jnp.int32, (key_width, LANES), 1) < half

    def keys_into(target_ref, c, lanes):
        near, away = [slots[min(2 * c + side, reach_blocks)] for side in (0, 1)]
        first_tile = stack_ref[near >> 1, :key_width, :]
        second_tile = stack_ref[away >> 1, :key_width, :]
        turned = pltpu.roll(jnp.where(left, second_tile, first_tile), half, 1)
        both = jnp.where(
            left, jnp.where((near & 1) == 0, first_tile, turned), jnp.where((away & 1) == 1, second_tile, turned)
        )
        target_ref[0, :key_width, lanes] = both
        target_ref[1, key_pad - key_width :, lanes] = both

    def index_keys_into(target_ref, w, at):
        start = pl.multiple_of(key_width + (slots[w] & 1) * half, half)
        target_ref[at : at + half, :] = stack_ref[slots[w] >> 1, pl.ds(start, half), :]

    main_ref[0, key_width:, :] = jnp.zeros((key_pad - key_width, reach), main_ref.dtype)
    main_ref[1, : key_pad - key_width, :] = jnp.zeros((key_pad - key_width, reach), main_ref.dtype)
    for c in range(reach // LANES):
        keys_into(main_ref, c, slice(c * LANES, (c + 1) * LANES))

    row_id = lax.broadcasted_iota(jnp.int32, (half, LANES), 0)
    lane_id = lax.broadcasted_iota(jnp.int32, (half, LANES), 1)
    own_low = (lane_id <= row_id) | (lane_id >= half) | jnp.logical_not(needed)
    bias = bias_ref[mine]

    heads = query_ref.shape[1] // key_width
    stacked_queries = []
    for parity in (0, 1):
        starts = [g * 2 * key_width + parity * (2 * key_width - key_pad) for g in range(heads // 2)]
        stacked_queries.append(lambda starts=starts: jnp.concatenate([query_ref[rows_here, at : at + key_pad] for at in starts], axis=0))

    def index_lhs(ref):
        return jnp.concatenate([ref[:, j * idim : (j + 1) * idim] for j in range(ref.shape[1] // idim - 1)], axis=0)

    if keep:
        for w in range(reach_blocks):
            index_keys_into(index_main, w, w * half)

    @pl.when(needed)
    def _():
        tail_ref[0, key_width:, :] = jnp.zeros((key_pad - key_width, LANES), tail_ref.dtype)
        tail_ref[1, : key_pad - key_width, :] = jnp.zeros((key_pad - key_width, LANES), tail_ref.dtype)
        keys_into(tail_ref, reach // LANES, slice(0, LANES))
        for parity in (0, 1):
            raw_ref[parity] = lax.dot_general(
                stacked_queries[parity](), tail_ref[parity], (((1,), (0,)), ((), ())), preferred_element_type=jnp.float32
            )
        if keep:
            index_keys_into(index_tail, reach_blocks, 0)
            index_tail[half:, :] = jnp.zeros((LANES - half, idim), index_tail.dtype)
            for k, ref in enumerate(index_query_refs):
                index_raw[k] = lax.dot_general(
                    index_lhs(ref), index_tail[...], (((1,), (1,)), ((), ())), preferred_element_type=jnp.float32
                )

    groups = 2 * max(1, heads // 2 // 4)
    each = heads // groups

    def matmul(k):
        parity = k % 2
        starts = [(g + k // 2 * each) * 2 * key_width + parity * (2 * key_width - key_pad) for g in range(each)]
        lhs = jnp.concatenate([query_ref[rows_here, at : at + key_pad] for at in starts], axis=0)
        main_raw[k % 2] = lax.dot_general(
            lhs, main_ref[parity], (((1,), (0,)), ((), ())), preferred_element_type=jnp.float32
        )

    def softmax(k, total):
        for g in range(each):
            tail = raw_ref[k % 2, (g + k // 2 * each) * half : (g + k // 2 * each + 1) * half, :]
            scores = ring_fold(own_low, main_raw[k % 2, g * half : (g + 1) * half, :], tail) + bias
            row_max = jnp.max(scores, axis=1, keepdims=True)
            powers = jnp.exp2((scores - row_max) * (score_scale * math.log2(math.e)))
            share = 1.0 / jnp.sum(powers, axis=1, keepdims=True)
            total = total + powers * share
        return total

    total = jnp.zeros((half, reach), jnp.float32)
    matmul(0)
    for k in range(1, groups + 1):
        if k < groups:
            matmul(k)
        total = softmax(k - 1, total)
    out_refs[0][...] = total

    if keep:
        total = jnp.zeros((half, reach), jnp.float32)
        for k, ref in enumerate(index_query_refs):
            lhs = index_lhs(ref)
            dots = lax.dot_general(lhs, index_main[...], (((1,), (1,)), ((), ())), preferred_element_type=jnp.float32)
            gains = ref[:, lhs.shape[0] // half * idim :].astype(jnp.float32)
            for j in range(lhs.shape[0] // half):
                here = slice(j * half, (j + 1) * half)
                folded = ring_fold(own_low, dots[here, :], index_raw[k, here, :])
                total = total + gains[:, j : j + 1] * jnp.maximum(folded, 0.0)
        out_refs[1][...] = jnp.where(bias == 0.0, total, 0.0)


def loss_kernel(sizes, bias_ref, *refs):
    half, total_heads = sizes
    value_refs, out_ref = refs[:-1], refs[-1]
    mine = own_block(True)
    visible = bias_ref[mine] == 0.0
    target = functools.reduce(jnp.add, [ref[0] for ref in value_refs]) * (1.0 / total_heads)
    index_score = functools.reduce(jnp.add, [ref[1] for ref in value_refs])
    masked = jnp.where(visible, index_score, hidden)
    row_max = jnp.max(masked, axis=1, keepdims=True)
    exp_sum = jnp.sum(jnp.where(visible, jnp.exp(masked - row_max), 0.0), axis=1, keepdims=True)
    positive = target > 0.0
    logs = jnp.log(jnp.where(positive, target, 1.0))
    entropy_sum = jnp.sum(jnp.where(positive, target * logs, 0.0), axis=1, keepdims=True)
    cross_sum = jnp.sum(jnp.where(visible, target * index_score, 0.0), axis=1, keepdims=True)
    target_sum = jnp.sum(target, axis=1, keepdims=True)
    column = entropy_sum - cross_sum + (row_max + jnp.log(exp_sum)) * target_sum
    rows = out_ref.shape[1]
    row_id = lax.broadcasted_iota(jnp.int32, (half, rows), 0)
    lane_id = lax.broadcasted_iota(jnp.int32, (half, rows), 1)
    out_ref[...] = jnp.sum(jnp.where(row_id + mine * half == lane_id, column, 0.0), axis=0, keepdims=True)


def per_device(
    latent_keys, index_keys, main_query, index_query, index_weight, segment_ids, block_order
):
    n_ctx, n_head = lax.axis_size("ctx"), lax.axis_size("head")
    rows, key_width = latent_keys.shape
    idim = index_keys.shape[1]
    seq_len = segment_ids.shape[0]
    half = seq_len // block_order.shape[0]
    reach = seq_len // 4
    heads = main_query.shape[1] // key_width
    key_pad = -(-key_width // LANES) * LANES
    vmem = pl.BlockSpec(memory_space=pltpu.VMEM)
    smem = pl.BlockSpec(memory_space=pltpu.SMEM)
    hbm = pl.BlockSpec(memory_space=pltpu.HBM)
    index_heads = index_weight.shape[1]

    def far(x):
        return pltpu.with_memory_space_constraint(x, pltpu.HBM)

    key_rows = (far(latent_keys.T), far(index_keys))
    small_vmem = pltpu.CompilerParams(vmem_limit_bytes=2 << 20)
    part = pl.pallas_call(
        part_kernel,
        out_shape=jax.ShapeDtypeStruct(((key_width + idim) // 2, rows), latent_keys.dtype),
        in_specs=[hbm, hbm],
        out_specs=vmem,
        scratch_shapes=[pltpu.SemaphoreType.DMA((2,))],
        compiler_params=small_vmem,
        name="part",
    )(*key_rows)
    packed = pl.pallas_call(
        pack_kernel,
        out_shape=jax.ShapeDtypeStruct((key_width + idim, rows), latent_keys.dtype),
        in_specs=[hbm, hbm],
        out_specs=vmem,
        scratch_shapes=[pltpu.SemaphoreType.DMA((2,))],
        compiler_params=small_vmem,
        name="pack",
    )(*key_rows)
    last = n_ctx // 2 - 1
    corner = swap(part, "ctx", 2 * last)
    own_core = []
    for s in reversed(range(1, last)):
        own_core.append(swap(packed, "ctx", 2 * s))
    corner_rest = swap(corner, "head", 1)
    pieces = []
    for piece in [packed] + own_core[::-1]:
        pieces += [piece, swap(piece, "ctx", 1)]
    pieces += [corner, corner_rest, swap(corner, "ctx", 1), swap(corner_rest, "ctx", 1)]
    seg_table = segment_ids.reshape(seq_len // LANES, LANES)

    copies = 8
    near_query = pl.pallas_call(
        load_kernel,
        out_shape=jax.ShapeDtypeStruct(main_query.shape, main_query.dtype),
        in_specs=[hbm],
        out_specs=vmem,
        scratch_shapes=[pltpu.SemaphoreType.DMA((copies,))],
        compiler_params=pltpu.CompilerParams(vmem_limit_bytes=12 << 20),
        cost_estimate=pl.CostEstimate(flops=1 << 10, bytes_accessed=10 << 20, transcendentals=0),
        name="load",
    )(far(main_query))
    index_row = (half, index_query.shape[1] + LANES)
    bias, keep_query, give_query = pl.pallas_call(
        functools.partial(prelude_kernel, (half, reach)),
        out_shape=(
            jax.ShapeDtypeStruct((2, half, reach), jnp.float32),
            jax.ShapeDtypeStruct(index_row, index_query.dtype),
            jax.ShapeDtypeStruct(index_row, index_query.dtype),
        ),
        in_specs=[hbm] * 4,
        out_specs=(vmem,) * 3,
        scratch_shapes=[
            pltpu.SMEM(block_order.shape, jnp.int32),
            pltpu.VMEM(seg_table.shape, jnp.int32),
            pltpu.VMEM((index_heads, rows), index_weight.dtype),
            pltpu.SemaphoreType.DMA((5,)),
        ],
        compiler_params=pltpu.CompilerParams(vmem_limit_bytes=12 << 20),
        cost_estimate=pl.CostEstimate(flops=1 << 20, bytes_accessed=1 << 20, transcendentals=0),
        name="prelude",
    )(far(block_order), far(seg_table), far(index_weight.T), far(index_query))
    taken_query = swap(give_query, "head", 1)

    stack = jax.ShapeDtypeStruct((n_ctx, key_width + idim, rows), packed.dtype)

    def block_sums(keep, keys):
        sums = jax.ShapeDtypeStruct((half, reach), jnp.float32)
        index_queries = [keep_query, taken_query] if keep else []
        return pl.pallas_call(
            functools.partial(block_kernel, (n_ctx, half, reach, key_width, idim), keep),
            out_shape=(sums, sums) if keep else (sums, stack),
            in_specs=[smem, smem] + [vmem] * (2 + len(index_queries) + len(keys)),
            out_specs=(vmem, vmem),
            scratch_shapes=[
                pltpu.VMEM((2, key_pad, reach), jnp.bfloat16),
                pltpu.VMEM((2, key_pad, LANES), jnp.bfloat16),
                pltpu.VMEM((reach, idim), jnp.bfloat16),
                pltpu.VMEM((LANES, idim), jnp.bfloat16),
                pltpu.VMEM((2, heads // 2 * half, LANES), jnp.float32),
                pltpu.VMEM((2, index_heads * half, LANES), jnp.float32),
                pltpu.VMEM((2, min(4, heads // 2) * half, reach), jnp.float32),
                pltpu.SMEM((block_order.shape[0],), jnp.int32),
            ],
            compiler_params=pltpu.CompilerParams(vmem_limit_bytes=28 << 20),
            cost_estimate=pl.CostEstimate(
                flops=2 * half * reach * heads * key_pad, bytes_accessed=4 << 20, transcendentals=0
            ),
            name="keep_sums" if keep else "give_sums",
        )(block_order, segment_ids, bias, near_query, *index_queries, *keys)

    given, key_stack = block_sums(False, pieces)
    kept, index_sums = block_sums(True, [key_stack])
    value = jnp.stack([kept + swap(given, "head", 1), index_sums])
    distances = [1 << k for k in range(1, n_head.bit_length() - 1)]
    for distance in distances[:-1]:
        value = value + swap(value, "head", distance)
    values = [value] + [swap(value, "head", distance) for distance in distances[-1:]]
    loss = pl.pallas_call(
        functools.partial(loss_kernel, (half, heads * n_head)),
        out_shape=jax.ShapeDtypeStruct((1, rows), jnp.float32),
        in_specs=[vmem] * (1 + len(values)),
        out_specs=vmem,
        compiler_params=pltpu.CompilerParams(vmem_limit_bytes=8 << 20),
        name="row_losses",
    )(bias, *values)
    return (loss + swap(loss, "head", 1)).reshape(rows)


def solution(mesh):
    in_specs = (
        P("ctx", None),
        P("ctx", None),
        P("ctx", "head"),
        P("ctx", "head"),
        P("ctx", "head"),
        P(),
        P(),
    )
    return jax.shard_map(per_device, mesh=mesh, in_specs=in_specs, out_specs=P("ctx"), check_vma=False)
```
